256 devices in a mesh: dp: 32 (over x, y, core), mp: 8 (over z).
Axes of the slice: x: 4, y: 4, z: 8, core: 2. Of those that a mesh axis runs over, the one named last changes fastest.
Arguments:
- features: bfloat16 [65536, 2, 512], P('dp'), may hold values from -27 to 27
- projection: bfloat16 [512, 256], replicated, may hold values from -1 to 1
- prototypes: float32 [3000, 256], P('mp'), may hold values from -7 to 7
Outputs:
- grad_prototypes: float32 [3000, 256], P('mp')
- grad_projection: float32 [512, 256], replicated
- loss: float32 [], replicated
The draws below stay inside these ranges and needn't reach their ends.
All inputs are finite; a program needn't handle non-finite values.
Results may differ from the reference program's by a relative error of at most 0.0019.
The reference program's roundings to bfloat16 on the way count: a program that leaves them out, or rounds other values in their place, can miss the bound.
Values may be sent and summed in bfloat16 or wider, within the bound.
A program may use at most 128 MiB of HBM per device.

```python
import math
import jax
import jax.numpy as jnp
from jax import lax

B_DEV = 2048
E = 512
P_SIZE = 256
K = 3000
ITERS = 3
WINDOW_BATCH = 65536


def shared_common(key):
    return jnp.clip(jax.random.normal(jax.random.fold_in(key, 101), (E,), jnp.float32), -3.0, 3.0)


def shared_direction(key):
    signs = jax.random.randint(jax.random.fold_in(key, 202), (P_SIZE,), 0, 2)
    return (2 * signs - 1).astype(jnp.float32) * (1.0 / math.sqrt(P_SIZE))


def draw_features(key, part):
    noise_key, scale_key, step_key, pick_key = jax.random.split(jax.random.fold_in(key, 303), 4)
    block_count = WINDOW_BATCH // B_DEV
    common = shared_common(key)[None, None, :]
    spread = jnp.exp(jax.random.uniform(scale_key, (block_count,), jnp.float32, math.log(1.0 / 3.0), 0.0))
    picked = jax.random.randint(pick_key, (), 0, block_count)
    block_scale = jnp.where(jnp.arange(block_count) == picked, 0.05, spread)
    scale_rows = jnp.repeat(block_scale, B_DEV, total_repeat_length=WINDOW_BATCH)[:, None, None]
    block_level = jax.random.uniform(step_key, (block_count,), jnp.float32, 0.0, 3.0)
    level_rows = jnp.repeat(block_level, B_DEV, total_repeat_length=WINDOW_BATCH)[:, None, None]
    noise_part = jnp.clip(jax.random.normal(noise_key, (WINDOW_BATCH, 2, E), jnp.float32), -6.0, 6.0)
    result = (noise_part + level_rows * common) * scale_rows
    return result.astype(jnp.bfloat16)


def draw_projection(key, part):
    noise = jnp.clip(jax.random.normal(jax.random.fold_in(key, 404), (E, P_SIZE), jnp.float32), -6.0, 6.0)
    common = shared_common(key)
    direction = shared_direction(key)
    result = noise * (1.0 / math.sqrt(E)) + common[:, None] * direction[None, :] * (math.sqrt(P_SIZE) / E)
    return result.astype(jnp.bfloat16)


def draw_prototypes(key, part):
    noise = jnp.clip(jax.random.normal(jax.random.fold_in(key, 505), (K, P_SIZE), jnp.float32), -6.0, 6.0)
    direction = shared_direction(key)
    rise = 0.4 * jnp.arange(K, dtype=jnp.float32) / (K - 1)
    result = noise + rise[:, None] * math.sqrt(P_SIZE) * direction[None, :]
    return result.astype(jnp.float32)


def setup_inputs(seed: int = 0) -> dict:
    key_of = jax.random.split(jax.random.key(seed), 4)
    features = draw_features(jax.random.fold_in(key_of[3], 71), 0)
    projection = draw_projection(jax.random.fold_in(key_of[3], 71), 0)
    prototypes = draw_prototypes(jax.random.fold_in(key_of[3], 71), 0)
    return dict(features=features, projection=projection, prototypes=prototypes)


EPSILON_CODES = 0.05
SOFTMAX_TEMPER = 0.1
LOSS_FACTOR = 4096.0
TINY = 1e-06
HIGH = lax.Precision.HIGHEST

def unit_rows(values):
    inverse = lax.rsqrt(lax.optimization_barrier(jnp.sum(values * values, axis=-1, keepdims=True)) + TINY)
    return (values * inverse, inverse)

def embed_block(block_feats, projection):
    raw_embed = jnp.einsum('bve,ep->bvp', block_feats.astype(jnp.float32), projection.astype(jnp.float32), precision=HIGH)
    return unit_rows(raw_embed)

def reference(features, projection, prototypes):
    proto_unit, proto_inverse = unit_rows(prototypes)
    proto_half = proto_unit.astype(jnp.bfloat16)
    proto_wide = proto_half.astype(jnp.float32)
    embed_all, unused_inverse = embed_block(features, projection)
    embed_all = embed_all.astype(jnp.bfloat16).astype(jnp.float32)
    prototype_logits = jnp.einsum('bvp,kp->bvk', embed_all, proto_wide, precision=HIGH)
    col_scale = jnp.ones((2, K), jnp.float32)
    row_scale = jnp.ones((WINDOW_BATCH, 2), jnp.float32)
    for iteration in range(ITERS):
        col_scale = 1.0 / jnp.einsum('bvk,bv->vk', jnp.exp(prototype_logits * (1.0 / EPSILON_CODES)), row_scale, precision=HIGH)
        row_scale = 1.0 / jnp.einsum('bvk,vk->bv', jnp.exp(prototype_logits * (1.0 / EPSILON_CODES)), col_scale, precision=HIGH)
    block_rows = math.gcd(WINDOW_BATCH, 4096)
    gradient_factor = LOSS_FACTOR / (2.0 * WINDOW_BATCH * SOFTMAX_TEMPER)

    def block_terms(totals, block_index):
        proto_acc, weight_acc, loss_running_sum = totals
        row_start = (block_index * block_rows).astype(jnp.int32)
        block_feats = lax.dynamic_slice_in_dim(features, row_start, block_rows, 0)
        embed_unit, embed_inverse = embed_block(block_feats, projection)
        embed_wide = embed_unit.astype(jnp.bfloat16).astype(jnp.float32)
        block_logits = lax.dynamic_slice_in_dim(prototype_logits, row_start, block_rows, 0)
        block_rowsc = lax.dynamic_slice_in_dim(row_scale, row_start, block_rows, 0)
        assignments = jnp.exp(block_logits * (1.0 / EPSILON_CODES)) * col_scale[None] * block_rowsc[..., None]
        softmax_exponent = jnp.exp(block_logits * (1.0 / SOFTMAX_TEMPER))
        softmax_denominator = lax.optimization_barrier(jnp.sum(softmax_exponent, axis=-1))
        swapped_targets = assignments[:, ::-1]
        grad_half = ((softmax_exponent / softmax_denominator[..., None] - swapped_targets) * gradient_factor).astype(jnp.bfloat16)
        grad_wide = grad_half.astype(jnp.float32)
        loss_running_sum = loss_running_sum + jnp.sum(swapped_targets * (block_logits * (1.0 / SOFTMAX_TEMPER) - jnp.log(softmax_denominator)[..., None]))
        proto_acc = proto_acc + jnp.einsum('bvk,bvp->kp', grad_wide, embed_wide, precision=HIGH)
        grad_unit = jnp.einsum('bvk,kp->bvp', grad_wide, proto_wide, precision=HIGH)
        along_unit = lax.optimization_barrier(jnp.sum(embed_unit * grad_unit, axis=-1, keepdims=True))
        grad_raw = ((grad_unit - embed_unit * along_unit) * embed_inverse).astype(jnp.bfloat16)
        weight_acc = weight_acc + jnp.einsum('bve,bvp->ep', block_feats.astype(jnp.float32), grad_raw.astype(jnp.float32), precision=HIGH)
        return ((proto_acc, weight_acc, loss_running_sum), None)
    initial = (jnp.zeros((K, P_SIZE), jnp.float32), jnp.zeros((E, P_SIZE), jnp.float32), jnp.zeros((), jnp.float32))
    totals, unused_out = lax.scan(block_terms, initial, jnp.arange(WINDOW_BATCH // block_rows, dtype=jnp.int32))
    proto_grad, weight_grad, loss_total = totals
    along_proto = lax.optimization_barrier(jnp.sum(proto_unit * proto_grad, axis=-1, keepdims=True))
    grad_protos = (proto_grad - proto_unit * along_proto) * proto_inverse
    loss_value = -loss_total / (2.0 * WINDOW_BATCH)
    return (grad_protos, weight_grad, loss_value)
```

```python
import functools

import jax
import jax.numpy as jnp
from jax import lax
from jax.experimental import pallas as pl
from jax.experimental.pallas import tpu as pltpu
from jax.sharding import PartitionSpec as P

MESH = pl.DeviceIdType.MESH
BF = jnp.bfloat16
F32 = jnp.float32

EPSILON_CODES = 0.05
SOFTMAX_TEMPER = 0.1
LOSS_FACTOR = 4096.0
TINY = 1e-06

NX, NY, NC, NZ = 4, 4, 2, 8
NP = NX * NY
KS = 375
KP = 384
LT = KP // 128
NT = NZ * LT
WR = 256
D = 256
E = 512
HALF = KP // 2
RH = D // 2
PR_ROWS = RH // NP
GR = E // 2 // NP
GRP = GR + 8
XY = [(dx, dy) for dx in range(NX) for dy in range(NY) if dx or dy]
ZO = [1, 7, 2, 6, 3, 5, 4]


def nt_dot(a, b):
    return lax.dot_general(a, b, (((1,), (1,)), ((), ())), preferred_element_type=F32)


def dot(a, b):
    return jnp.dot(a, b, preferred_element_type=F32)


def kernel(
    batch_rows,
    feats, weight, protos,
    gproto_out, gweight_out, loss_out,
    pu, ph, unit, inv, emb, embt, xt,
    ex, sc, so, den, acc, vec, csum, cothers, gm,
    buf_a, buf_b, vec_b,
    eg, pg, buf_p, pr, buf_q, pq, buf_z, fg, gw, buf_w, gwr, buf_x, buf_y, fw, loss_acc,
    s_z, r_z, s_f, r_f, s_e, r_e, s_a, r_a, s_b, r_b, s_c, r_c,
    s_p, r_p, s_q, r_q, s_qz, r_qz, s_qg, r_qg, s_qc, r_qc,
    s_w, r_w, s_wx, r_wx, s_wz, r_wz, s_wg, r_wg, s_wc, r_wc,
):
    dp = lax.axis_index("dp")
    z = lax.axis_index("mp")
    x, y, c = dp // (NY * NC), (dp // NC) % NY, dp % NC
    o = 1 - c
    me_p = x * NY + y
    gf = LOSS_FACTOR / (2.0 * batch_rows * SOFTMAX_TEMPER)
    pending = []

    def plane(dx, dy):
        px, py = (x + dx) % NX, (y + dy) % NY
        return px * NY + py

    def plane_dev(p):
        return {"dp": p * NC + c, "mp": z}

    def z_dev(dz):
        return {"dp": dp, "mp": (z + dz) % NZ}

    sibling = {"dp": dp + 1 - 2 * c, "mp": z}

    def send(src, dst, ssem, rsem, device):
        copy = pltpu.make_async_remote_copy(
            src_ref=src, dst_ref=dst, send_sem=ssem, recv_sem=rsem, device_id=device, device_id_type=MESH
        )
        copy.start()
        pending.append(copy)
        return copy

    barrier = pltpu.get_barrier_semaphore()
    pl.semaphore_signal(barrier, inc=1, device_id=sibling, device_id_type=MESH)
    for dx, dy in XY:
        pl.semaphore_signal(barrier, inc=1, device_id=plane_dev(plane(dx, dy)), device_id_type=MESH)
    for dz in ZO:
        pl.semaphore_signal(barrier, inc=1, device_id=z_dev(dz), device_id_type=MESH)

    pu[...] = jnp.zeros_like(pu)
    own = protos[...]
    pu[0:KS, :] = own * lax.rsqrt(jnp.sum(own * own, axis=-1, keepdims=True) + TINY)
    ph[z] = pu[...].astype(BF)
    pl.semaphore_wait(barrier, 1 + len(XY) + len(ZO))

    zcopies = {}
    for i, dz in enumerate(ZO):
        part = ph.at[z, pl.ds(pl.multiple_of(c * HALF, HALF), HALF)]
        zcopies[dz] = send(part, part, s_z.at[i], r_z.at[i], z_dev(dz))

    def embed(view, row, erow):
        raw = dot(feats[view], weight[...])
        inverse = lax.rsqrt(jnp.sum(raw * raw, axis=-1, keepdims=True) + TINY)
        u = raw * inverse
        inv[row : row + WR, :] = inverse
        unit[row : row + WR, :] = u
        emb[erow : erow + WR, :] = u.astype(BF)

    embed(o, WR, 2 * WR)
    ecopy = send(emb.at[pl.ds(2 * WR, WR)], emb.at[pl.ds(WR, WR)], s_e, r_e, sibling)
    embed(c, 0, 0)
    ecopy.wait_recv()

    def scores_slab(q):
        pq_ = ph[q]
        tot = jnp.zeros((8, KP), F32)
        for b in range(2):
            s = nt_dot(emb[b * WR : (b + 1) * WR, :], pq_)
            e = jnp.exp(s * (1.0 / EPSILON_CODES))
            ex[q, b * WR : (b + 1) * WR, :] = e
            if b == 0:
                sc[q, 0:WR, :] = s
            tot = tot + jnp.sum(e.reshape(WR // 8, 8, KP), axis=0)
        acc[q] = tot

    scores_slab(z)
    for i, dz in enumerate(ZO):
        q = (z + NZ - dz) % NZ
        zcopies[dz].wait_recv()
        part = ph.at[q, pl.ds(pl.multiple_of(c * HALF, HALF), HALF)]
        fwd = send(part, part, s_f.at[i], r_f.at[i], sibling)
        fwd.wait_recv()
        scores_slab(q)

    lane = lax.broadcasted_iota(jnp.int32, (NT, 128), 1)
    row = lax.broadcasted_iota(jnp.int32, (NT, 128), 0)
    valid = lane + (row % LT) * 128 < KS

    def finish_column_sums(k):
        for q in range(NZ):
            part = jnp.sum(acc[q], axis=0, keepdims=True)
            for j in range(LT):
                vec[k, q * LT + j : q * LT + j + 1, :] = part[:, j * 128 : (j + 1) * 128]

    def reduce_columns(k, work_a, work_b):
        finish_column_sums(k)
        copies = []
        for i, (dx, dy) in enumerate(XY):
            copies.append(
                send(vec.at[k], buf_a.at[k, i], s_a.at[k, i], r_a.at[k, i], plane_dev(plane(dx, dy)))
            )
        work_a()
        total = vec[k]
        for i, copy in enumerate(copies):
            copy.wait_recv()
            total = total + buf_a[k, i]
        vec_b[k] = total
        copies = []
        for i, dz in enumerate(ZO):
            copies.append(send(vec_b.at[k], buf_b.at[k, i], s_b.at[k, i], r_b.at[k, i], z_dev(dz)))
        work_b()
        for i, copy in enumerate(copies):
            copy.wait_recv()
            total = total + buf_b[k, i]
        csum[k] = jnp.where(valid, 1.0 / total, 0.0)

    def other_view():
        def step(q, carry):
            s = nt_dot(emb[2 * WR : 3 * WR, :], ph[q])
            ex[q, 2 * WR : 3 * WR, :] = jnp.exp(s * (1.0 / EPSILON_CODES))
            sc[q, WR : 2 * WR, :] = s
            return carry

        lax.fori_loop(0, NZ, step, 0)

    last = lax.broadcasted_iota(jnp.int32, (1, 128), 1) < KS - (LT - 1) * 128

    def denominators(first):
        R = 64

        def step(b, carry):
            rows = pl.ds(pl.multiple_of(first + b * R, R), R)
            total = jnp.zeros((R, 128), F32)
            for q in range(NZ):
                s = jnp.exp(sc[q, rows, :] * (1.0 / SOFTMAX_TEMPER))
                so[q, rows, :] = s
                for j in range(LT):
                    part = s[:, j * 128 : (j + 1) * 128]
                    if j == LT - 1:
                        part = jnp.where(last, part, 0.0)
                    total = total + part
            den[rows, :] = jnp.sum(total, axis=1, keepdims=True)
            return carry

        lax.fori_loop(0, WR // R, step, 0)

    def transposes():
        embt[:, 0:WR] = emb[0:WR, :].astype(F32).T.astype(BF)
        embt[:, WR : 2 * WR] = emb[2 * WR : 3 * WR, :].astype(F32).T.astype(BF)

    def transposes_x():
        xt[:, 0:WR] = feats[c].astype(F32).T.astype(BF)
        xt[:, WR : 2 * WR] = feats[o].astype(F32).T.astype(BF)

    def row_inverse(cs, rows, R):
        total = jnp.zeros((R, 128), F32)
        for q in range(NZ):
            for j in range(LT):
                t = q * LT + j
                total = total + ex[q, rows, j * 128 : (j + 1) * 128] * cs[t : t + 1, :]
        return 1.0 / jnp.sum(total, axis=1, keepdims=True)

    def sinkhorn_pass(k):
        R = 64
        acc[...] = jnp.zeros_like(acc)

        def step(b, carry):
            rows = pl.ds(pl.multiple_of(b * R, R), R)
            r = row_inverse(csum.at[k], rows, R)
            for q in range(NZ):
                t = ex[q, rows, :] * r
                acc[q] += jnp.sum(t.reshape(R // 8, 8, KP), axis=0)
            return carry

        lax.fori_loop(0, 2 * WR // R, step, 0)

    def nothing():
        pass

    reduce_columns(0, other_view, lambda: denominators(0))
    sinkhorn_pass(0)
    reduce_columns(1, lambda: denominators(WR), transposes)
    sinkhorn_pass(1)
    reduce_columns(2, transposes_x, nothing)
    ccopy = send(csum.at[2], cothers, s_c, r_c, sibling)
    ccopy.wait_recv()

    RG = 32
    loss_acc[...] = jnp.zeros_like(loss_acc)

    def grad_step(b, carry):
        rows_c = pl.ds(pl.multiple_of(b * RG, RG), RG)
        rows_o = pl.ds(pl.multiple_of(WR + b * RG, RG), RG)
        erows_o = pl.ds(pl.multiple_of(2 * WR + b * RG, RG), RG)
        rc = row_inverse(csum.at[2], rows_c, RG) * gf
        ro = row_inverse(cothers, erows_o, RG) * gf
        dc = gf / den[rows_c, :]
        do = gf / den[rows_o, :]
        total = jnp.zeros((RG, 128), F32)
        for q in range(NZ):
            for j in range(LT):
                t = q * LT + j
                cols = slice(j * 128, (j + 1) * 128)
                ac = ex[q, rows_c, cols] * csum[2, t : t + 1, :] * rc
                ao = ex[q, erows_o, cols] * cothers[t : t + 1, :] * ro
                gm[q, rows_c, cols] = (so[q, rows_c, cols] * dc - ao).astype(BF)
                gm[q, rows_o, cols] = (so[q, rows_o, cols] * do - ac).astype(BF)
                total = total + ao * sc[q, rows_c, cols] + ac * sc[q, rows_o, cols]
        loss_acc[...] += jnp.sum(total.reshape(RG // 8, 8, 128), axis=0)
        return carry

    lax.fori_loop(0, WR // RG, grad_step, 0)

    eg[...] = jnp.zeros_like(eg)
    pcopies = []
    for q in range(NZ):
        pg[q] = dot(embt[...], gm[q])
        pcopies.append(
            send(pg.at[q, pl.ds(pl.multiple_of(o * RH, RH), RH)], buf_p.at[q], s_p.at[q], r_p.at[q], sibling)
        )
    for q in range(NZ):
        pcopies[q].wait_recv()
        pr[q] = pg[q, pl.ds(pl.multiple_of(c * RH, RH), RH), :] + buf_p[q]
    qcopies = []
    for i, (dx, dy) in enumerate(XY):
        p = plane(dx, dy)
        qcopies.append(
            send(
                pr.at[:, pl.ds(pl.multiple_of(p * PR_ROWS, PR_ROWS), PR_ROWS)],
                buf_q.at[i], s_q.at[i], r_q.at[i], plane_dev(p),
            )
        )

    for q in range(NZ):
        eg[...] += dot(gm[q], ph[q])
    along = jnp.sum(unit[...] * eg[...], axis=-1, keepdims=True)
    graw = ((eg[...] - unit[...] * along) * inv[...]).astype(BF)
    gfull = dot(xt[...], graw)
    for h in range(NC):
        for p in range(NP):
            first = h * (E // 2) + p * GR
            gw[h, p, 0:GR, :] = gfull[first : first + GR, :]
            gw[h, p, GR:GRP, :] = jnp.zeros((GRP - GR, D), F32)
    log_total = jnp.sum(jnp.log(den[...]))
    soft_total = jnp.sum(loss_acc[...]) * (1.0 / (SOFTMAX_TEMPER * gf))
    gw[0, 0, GR:GRP, :] = jnp.full((GRP - GR, D), soft_total - log_total, F32)
    wcopy = send(gw.at[o], buf_w, s_w, r_w, sibling)
    wcopy.wait_recv()
    gwr[...] = gw[c] + buf_w[...]
    wcopies = []
    for i, (dx, dy) in enumerate(XY):
        p = plane(dx, dy)
        wcopies.append(send(gwr.at[p], buf_x.at[i], s_wx.at[i], r_wx.at[i], plane_dev(p)))

    total = pr[:, pl.ds(pl.multiple_of(me_p * PR_ROWS, PR_ROWS), PR_ROWS), :]
    for i, copy in enumerate(qcopies):
        copy.wait_recv()
        total = total + buf_q[i]
    pq[...] = total
    zc = []
    for i, dz in enumerate(ZO):
        q = (z + dz) % NZ
        zc.append(send(pq.at[q], buf_z.at[i], s_qz.at[i], r_qz.at[i], z_dev(dz)))

    total = gwr[me_p]
    for i, copy in enumerate(wcopies):
        copy.wait_recv()
        total = total + buf_x[i]
    buf_y[z] = total
    wz = []
    for i, dz in enumerate(ZO):
        wz.append(send(buf_y.at[z], buf_y.at[z], s_wz.at[i], r_wz.at[i], z_dev(dz)))

    total = pq[z]
    for i, copy in enumerate(zc):
        copy.wait_recv()
        total = total + buf_z[i]
    fg[c, me_p] = total
    qg = []
    for i, (dx, dy) in enumerate(XY):
        qg.append(
            send(fg.at[c, me_p], fg.at[c, me_p], s_qg.at[i], r_qg.at[i], plane_dev(plane(dx, dy)))
        )

    for copy in wz:
        copy.wait_recv()
    total = buf_y[0]
    for k in range(1, NZ):
        total = total + buf_y[k]
    fw[c, me_p] = total
    wg = []
    for i, (dx, dy) in enumerate(XY):
        wg.append(
            send(fw.at[c, me_p], fw.at[c, me_p], s_wg.at[i], r_wg.at[i], plane_dev(plane(dx, dy)))
        )

    for copy in qg:
        copy.wait_recv()
    qc = send(fg.at[c], fg.at[c], s_qc, r_qc, sibling)
    qc.wait_recv()
    g = fg[...].reshape(D, KP).T
    u = pu[...]
    along_p = jnp.sum(u * g, axis=-1, keepdims=True)
    own = protos[...]
    pinv = lax.rsqrt(jnp.sum(own * own, axis=-1, keepdims=True) + TINY)
    gproto_out[...] = (g - u * along_p)[0:KS, :] * pinv

    for copy in wg:
        copy.wait_recv()
    wc = send(fw.at[c], fw.at[c], s_wc, r_wc, sibling)
    wc.wait_recv()
    for h in range(NC):
        for p in range(NP):
            first = h * (E // 2) + p * GR
            gweight_out[first : first + GR, :] = fw[h, p, 0:GR, :]
    loss_out[...] = fw[0, 0, GR:GRP, 0:128] * (-1.0 / (2.0 * batch_rows))

    for copy in pending:
        copy.wait_send()


def body(features, projection, prototypes):
    rows = features.shape[0]
    batch_rows = rows * lax.axis_size("dp")
    first = lax.axis_index("mp") * WR
    feats = lax.dynamic_slice_in_dim(features, first, WR, 0).transpose(1, 0, 2)
    dma = pltpu.SemaphoreType.DMA
    nxy, nz = len(XY), len(ZO)
    vm = pltpu.VMEM
    scratch = [
        vm((KP, D), F32), vm((NZ, KP, D), BF), vm((2 * WR, D), F32), vm((2 * WR, 1), F32),
        vm((3 * WR, D), BF), vm((D, 2 * WR), BF), vm((E, 2 * WR), BF),
        vm((NZ, 3 * WR, KP), F32), vm((NZ, 2 * WR, KP), F32), vm((NZ, 2 * WR, KP), F32),
        vm((2 * WR, 1), F32), vm((NZ, 8, KP), F32), vm((3, NT, 128), F32), vm((3, NT, 128), F32),
        vm((NT, 128), F32), vm((NZ, 2 * WR, KP), BF),
        vm((3, nxy, NT, 128), F32), vm((3, nz, NT, 128), F32), vm((3, NT, 128), F32),
        vm((2 * WR, D), F32), vm((NZ, D, KP), F32), vm((NZ, RH, KP), F32), vm((NZ, RH, KP), F32),
        vm((nxy, NZ, PR_ROWS, KP), F32), vm((NZ, PR_ROWS, KP), F32), vm((nz, PR_ROWS, KP), F32),
        vm((NC, NP, PR_ROWS, KP), F32), vm((NC, NP, GRP, D), F32), vm((NP, GRP, D), F32),
        vm((NP, GRP, D), F32), vm((nxy, GRP, D), F32), vm((NZ, GRP, D), F32), vm((NC, NP, GRP, D), F32),
        vm((8, 128), F32),
        dma((nz,)), dma((nz,)), dma((nz,)), dma((nz,)), dma, dma,
        dma((3, nxy)), dma((3, nxy)), dma((3, nz)), dma((3, nz)), dma, dma,
        dma((NZ,)), dma((NZ,)), dma((nxy,)), dma((nxy,)), dma((nz,)), dma((nz,)),
        dma((nxy,)), dma((nxy,)), dma, dma,
        dma, dma, dma((nxy,)), dma((nxy,)), dma((nz,)), dma((nz,)), dma((nxy,)), dma((nxy,)), dma, dma,
    ]
    vspec = pl.BlockSpec(memory_space=pltpu.VMEM)
    gproto, gweight, loss = pl.pallas_call(
        functools.partial(kernel, batch_rows),
        out_shape=(
            jax.ShapeDtypeStruct((KS, D), F32),
            jax.ShapeDtypeStruct((E, D), F32),
            jax.ShapeDtypeStruct((8, 128), F32),
        ),
        in_specs=[vspec] * 3,
        out_specs=(vspec,) * 3,
        scratch_shapes=scratch,
        compiler_params=pltpu.CompilerParams(
            collective_id=0, has_side_effects=True, vmem_limit_bytes=60 * 1024 * 1024
        ),
        name="swav",
    )(feats, projection, prototypes)
    return gproto, gweight, loss[0, 0]


def solution(mesh):
    return jax.shard_map(
        body,
        mesh=mesh,
        in_specs=(P("dp", None, None), P(), P("mp", None)),
        out_specs=(P("mp", None), P(), P()),
        check_vma=False,
    )
```

```python
import functools

import jax
import jax.numpy as jnp
from jax import lax
from jax.experimental import pallas as pl
from jax.experimental.pallas import tpu as pltpu
from jax.sharding import PartitionSpec as P

MESH = pl.DeviceIdType.MESH
BF = jnp.bfloat16
F32 = jnp.float32

EPSILON_CODES = 0.05
SOFTMAX_TEMPER = 0.1
LOSS_FACTOR = 4096.0
VLIM = 60
TINY = 1e-06

NX, NY, NC, NZ = 4, 4, 2, 8
NP = NX * NY
KS = 375
KP = 384
LT = KP // 128
NT = NZ * LT
WR = 256
D = 256
E = 512
HALF = KP // 2
RH = D // 2
PR_ROWS = RH // NP
GR = E // 2 // NP
GH = E // 2
XL = 256
GRPS = 4
ORD = [4, 3, 5, 2, 6, 1, 7, 0]
XY = [(dx, dy) for dx in range(NX) for dy in range(NY) if dx or dy]
ZO = [1, 7, 2, 6, 3, 5, 4]


def nt_dot(a, b):
    return lax.dot_general(a, b, (((1,), (1,)), ((), ())), preferred_element_type=F32)


def dot(a, b):
    return jnp.dot(a, b, preferred_element_type=F32)


def kernel(
    batch_rows,
    feats_in, weight_in, protos_in,
    gproto_out, gweight_out,
    raw, feats, weight, protos, s_in,
    pu, ph, unit, inv, emb, embt, xt,
    ex, sc, so, den, acc, vec, csum, cothers, gm,
    buf_a, buf_b, vec_b,
    eg, pg, buf_p, pr, buf_q, pq, buf_z, buf_f, zs, buf_xz, fg, gw, buf_w, gwr, buf_x, buf_y, fw, loss_acc,
    s_z, r_z, s_f, r_f, s_e, r_e, s_a, r_a, s_b, r_b, s_c, r_c,
    s_p, r_p, s_q, r_q, s_zf, r_zf, s_xz, r_xz, s_qz, r_qz, s_qg, r_qg, s_qc, r_qc,
    s_w, r_w, s_wx, r_wx, s_wz, r_wz, s_wg, r_wg, s_wc, r_wc,
):
    dp = lax.axis_index("dp")
    z = lax.axis_index("mp")
    x, y, c = dp // (NY * NC), (dp // NC) % NY, dp % NC
    o = 1 - c
    me_p = x * NY + y
    gf = LOSS_FACTOR / (2.0 * batch_rows * SOFTMAX_TEMPER)
    pending = []

    def plane(dx, dy):
        px, py = (x + dx) % NX, (y + dy) % NY
        return px * NY + py

    def plane_dev(p):
        return {"dp": p * NC + c, "mp": z}

    def z_dev(dz):
        return {"dp": dp, "mp": (z + dz) % NZ}

    sibling = {"dp": dp + 1 - 2 * c, "mp": z}

    def send(src, dst, ssem, rsem, device):
        copy = pltpu.make_async_remote_copy(
            src_ref=src, dst_ref=dst, send_sem=ssem, recv_sem=rsem, device_id=device, device_id_type=MESH
        )
        copy.start()
        pending.append(copy)
        return copy

    def arrival(dst, ssem, rsem):
        return pltpu.make_async_remote_copy(
            src_ref=dst, dst_ref=dst, send_sem=ssem, recv_sem=rsem, device_id=sibling, device_id_type=MESH
        )

    def zf_recv(dz):
        k = (z + dz) % NZ
        return arrival(buf_f.at[k], s_zf.at[0], r_zf.at[k])

    def wz_recv(dz):
        k = (z + dz) % NZ
        return arrival(buf_y.at[k], s_wz.at[0], r_wz.at[k])

    barrier = pltpu.get_barrier_semaphore()
    pl.semaphore_signal(barrier, inc=1, device_id=sibling, device_id_type=MESH)
    for dx, dy in XY:
        pl.semaphore_signal(barrier, inc=1, device_id=plane_dev(plane(dx, dy)), device_id_type=MESH)
    for dz in ZO:
        pl.semaphore_signal(barrier, inc=1, device_id=z_dev(dz), device_id_type=MESH)

    loads = [
        pltpu.make_async_copy(protos_in, protos, s_in.at[0]),
        pltpu.make_async_copy(feats_in.at[pl.ds(z * WR, WR)], raw, s_in.at[1]),
        pltpu.make_async_copy(weight_in, weight, s_in.at[2]),
    ]
    for load in loads:
        load.start()

    loads[0].wait()
    pu[...] = jnp.zeros_like(pu)
    own = protos[...]
    pu[0:KS, :] = own * lax.rsqrt(jnp.sum(own * own, axis=-1, keepdims=True) + TINY)
    ph[z] = pu[...].astype(BF)
    pl.semaphore_wait(barrier, 1 + len(XY) + len(ZO))

    zcopies = {}
    for i, dz in enumerate(ZO):
        part = ph.at[z, pl.ds(pl.multiple_of(c * HALF, HALF), HALF)]
        zcopies[dz] = send(part, part, s_z.at[i], r_z.at[i], z_dev(dz))

    loads[1].wait()
    loads[2].wait()
    to = lax.broadcasted_iota(jnp.int32, (2 * WR, 2 * WR), 0)
    fro = lax.broadcasted_iota(jnp.int32, (2 * WR, 2 * WR), 1)
    order = ((to % WR) * 2 + to // WR == fro).astype(F32).astype(BF)
    feats[...] = dot(order, raw[...].reshape(2 * WR, E)).astype(BF).reshape(2, WR, E)

    def embed(view, row, erow):
        raw = dot(feats[view], weight[...])
        inverse = lax.rsqrt(jnp.sum(raw * raw, axis=-1, keepdims=True) + TINY)
        u = raw * inverse
        inv[row : row + WR, :] = inverse
        unit[row : row + WR, :] = u
        emb[erow : erow + WR, :] = u.astype(BF)

    embed(o, WR, 2 * WR)
    ecopy = send(emb.at[pl.ds(2 * WR, WR)], emb.at[pl.ds(WR, WR)], s_e, r_e, sibling)
    embed(c, 0, 0)
    ecopy.wait_recv()

    def scores_slab(q):
        pq_ = ph[q]
        tot = jnp.zeros((8, KP), F32)
        for b in range(2):
            s = nt_dot(emb[b * WR : (b + 1) * WR, :], pq_)
            e = jnp.exp(s * (1.0 / EPSILON_CODES))
            ex[q, b * WR : (b + 1) * WR, :] = e
            if b == 0:
                sc[q, 0:WR, :] = s
            tot = tot + jnp.sum(e.reshape(WR // 8, 8, KP), axis=0)
        acc[q] = tot

    scores_slab(z)
    for i, dz in enumerate(ZO):
        q = (z + NZ - dz) % NZ
        zcopies[dz].wait_recv()
        part = ph.at[q, pl.ds(pl.multiple_of(c * HALF, HALF), HALF)]
        fwd = send(part, part, s_f.at[i], r_f.at[i], sibling)
        fwd.wait_recv()
        scores_slab(q)

    lane = lax.broadcasted_iota(jnp.int32, (NT, 128), 1)
    row = lax.broadcasted_iota(jnp.int32, (NT, 128), 0)
    valid = lane + (row % LT) * 128 < KS

    def finish_column_sums(k):
        for q in range(NZ):
            part = jnp.sum(acc[q], axis=0, keepdims=True)
            for j in range(LT):
                vec[k, q * LT + j : q * LT + j + 1, :] = part[:, j * 128 : (j + 1) * 128]

    def reduce_columns(k, work_a, work_b):
        finish_column_sums(k)
        copies = []
        for i, (dx, dy) in enumerate(XY):
            copies.append(
                send(vec.at[k], buf_a.at[k, i], s_a.at[k, i], r_a.at[k, i], plane_dev(plane(dx, dy)))
            )
        work_a()
        total = vec[k]
        for i, copy in enumerate(copies):
            copy.wait_recv()
            total = total + buf_a[k, i]
        vec_b[k] = total
        copies = []
        for i, dz in enumerate(ZO):
            copies.append(send(vec_b.at[k], buf_b.at[k, i], s_b.at[k, i], r_b.at[k, i], z_dev(dz)))
        work_b()
        for i, copy in enumerate(copies):
            copy.wait_recv()
            total = total + buf_b[k, i]
        csum[k] = jnp.where(valid, 1.0 / total, 0.0)

    def other_view():
        def step(q, carry):
            s = nt_dot(emb[2 * WR : 3 * WR, :], ph[q])
            ex[q, 2 * WR : 3 * WR, :] = jnp.exp(s * (1.0 / EPSILON_CODES))
            sc[q, WR : 2 * WR, :] = s
            return carry

        lax.fori_loop(0, NZ, step, 0)

    last = lax.broadcasted_iota(jnp.int32, (1, 128), 1) < KS - (LT - 1) * 128

    def denominators(first):
        R = 64

        def step(b, carry):
            rows = pl.ds(pl.multiple_of(first + b * R, R), R)
            total = jnp.zeros((R, 128), F32)
            for q in range(NZ):
                s = jnp.exp(sc[q, rows, :] * (1.0 / SOFTMAX_TEMPER))
                so[q, rows, :] = s
                for j in range(LT):
                    part = s[:, j * 128 : (j + 1) * 128]
                    if j == LT - 1:
                        part = jnp.where(last, part, 0.0)
                    total = total + part
            den[rows, :] = jnp.sum(total, axis=1, keepdims=True)
            return carry

        lax.fori_loop(0, WR // R, step, 0)

    def transposes():
        embt[:, 0:WR] = emb[0:WR, :].astype(F32).T.astype(BF)
        embt[:, WR : 2 * WR] = emb[2 * WR : 3 * WR, :].astype(F32).T.astype(BF)

    def transposes_x():
        xt[:, 0:WR] = feats[c].astype(F32).T.astype(BF)
        xt[:, WR : 2 * WR] = feats[o].astype(F32).T.astype(BF)

    def row_inverse(cs, rows, R):
        total = jnp.zeros((R, 128), F32)
        for q in range(NZ):
            for j in range(LT):
                t = q * LT + j
                total = total + ex[q, rows, j * 128 : (j + 1) * 128] * cs[t : t + 1, :]
        return 1.0 / jnp.sum(total, axis=1, keepdims=True)

    def sinkhorn_pass(k):
        R = 64
        acc[...] = jnp.zeros_like(acc)

        def step(b, carry):
            rows = pl.ds(pl.multiple_of(b * R, R), R)
            r = row_inverse(csum.at[k], rows, R)
            for q in range(NZ):
                t = ex[q, rows, :] * r
                acc[q] += jnp.sum(t.reshape(R // 8, 8, KP), axis=0)
            return carry

        lax.fori_loop(0, 2 * WR // R, step, 0)

    def nothing():
        pass

    reduce_columns(0, other_view, lambda: denominators(0))
    sinkhorn_pass(0)
    reduce_columns(1, lambda: denominators(WR), transposes)
    sinkhorn_pass(1)
    reduce_columns(2, transposes_x, nothing)
    ccopy = send(csum.at[2], cothers, s_c, r_c, sibling)
    ccopy.wait_recv()

    RG = 32
    loss_acc[...] = jnp.zeros_like(loss_acc)

    def grad_step(b, carry):
        rows_c = pl.ds(pl.multiple_of(b * RG, RG), RG)
        rows_o = pl.ds(pl.multiple_of(WR + b * RG, RG), RG)
        erows_o = pl.ds(pl.multiple_of(2 * WR + b * RG, RG), RG)
        rc = row_inverse(csum.at[2], rows_c, RG) * gf
        ro = row_inverse(cothers, erows_o, RG) * gf
        dc = gf / den[rows_c, :]
        do = gf / den[rows_o, :]
        total = jnp.zeros((RG, 128), F32)
        for q in range(NZ):
            for j in range(LT):
                t = q * LT + j
                cols = slice(j * 128, (j + 1) * 128)
                ac = ex[q, rows_c, cols] * csum[2, t : t + 1, :] * rc
                ao = ex[q, erows_o, cols] * cothers[t : t + 1, :] * ro
                gm[q, rows_c, cols] = (so[q, rows_c, cols] * dc - ao).astype(BF)
                gm[q, rows_o, cols] = (so[q, rows_o, cols] * do - ac).astype(BF)
                total = total + ao * sc[q, rows_c, cols] + ac * sc[q, rows_o, cols]
        loss_acc[...] += jnp.sum(total.reshape(RG // 8, 8, 128), axis=0)
        return carry

    lax.fori_loop(0, WR // RG, grad_step, 0)

    log_total = jnp.sum(jnp.log(den[...]))
    share = jnp.sum(loss_acc[...]) * (1.0 / (SOFTMAX_TEMPER * gf)) - log_total
    spare = lax.broadcasted_iota(jnp.int32, (8, 128), 1) == 127

    pcopies = []
    for i, dz in enumerate(ORD):
        q = (z + dz) % NZ
        pg[i] = dot(embt[...], gm[q])
        pg[i, 0:8, KP - 128 : KP] = jnp.where(spare, share, pg[i, 0:8, KP - 128 : KP])
        pcopies.append(
            send(pg.at[i, pl.ds(pl.multiple_of(o * RH, RH), RH)], buf_p.at[i], s_p.at[i], r_p.at[i], sibling)
        )
    eg[...] = jnp.zeros_like(eg)
    qcopies = []
    zf = []
    for i, dz in enumerate(ORD):
        q = (z + dz) % NZ
        pcopies[i].wait_recv()
        pr[i] = pg[i, pl.ds(pl.multiple_of(c * RH, RH), RH), :] + buf_p[i]
        if dz:
            zf.append(
                send(pr.at[i, :, pl.ds(XL, KP - XL)], buf_f.at[z], s_zf.at[i], r_zf.at[z], z_dev(dz))
            )
        else:
            buf_f[z] = pr[i, :, XL:KP]
        eg[...] += dot(gm[q], ph[q])
        if i % GRPS == GRPS - 1:
            g = i // GRPS
            for n, (dx, dy) in enumerate(XY):
                p = plane(dx, dy)
                qcopies.append(
                    send(
                        pr.at[pl.ds(g * GRPS, GRPS), pl.ds(pl.multiple_of(p * PR_ROWS, PR_ROWS), PR_ROWS), pl.ds(0, XL)],
                        buf_q.at[n, pl.ds(g * GRPS, GRPS)], s_q.at[g, n], r_q.at[g, n], plane_dev(p),
                    )
                )

    along = jnp.sum(unit[...] * eg[...], axis=-1, keepdims=True)
    graw = ((eg[...] - unit[...] * along) * inv[...]).astype(BF)
    gw[...] = dot(xt[...], graw)
    wcopy = send(gw.at[pl.ds(pl.multiple_of(o * GH, GH), GH)], buf_w, s_w, r_w, sibling)
    wcopy.wait_recv()
    gwr[...] = gw[pl.ds(pl.multiple_of(c * GH, GH), GH), :] + buf_w[...]
    wcopies = []
    for i, (dx, dy) in enumerate(XY):
        p = plane(dx, dy)
        wcopies.append(
            send(gwr.at[pl.ds(pl.multiple_of(p * GR, GR), GR)], buf_x.at[i], s_wx.at[i], r_wx.at[i], plane_dev(p))
        )

    for i, dz in enumerate(ORD):
        if dz:
            zf_recv(dz).wait_recv()
    total = buf_f[0]
    for k in range(1, NZ):
        total = total + buf_f[k]
    zs[...] = total
    xz = []
    for i, (dx, dy) in enumerate(XY):
        p = plane(dx, dy)
        xz.append(
            send(zs.at[pl.ds(pl.multiple_of(p * PR_ROWS, PR_ROWS), PR_ROWS)], buf_xz.at[i], s_xz.at[i], r_xz.at[i], plane_dev(p))
        )

    total = gwr[pl.ds(pl.multiple_of(me_p * GR, GR), GR), :]
    for i, copy in enumerate(wcopies):
        copy.wait_recv()
        total = total + buf_x[i]
    buf_y[z] = total
    wz = []
    for i, dz in enumerate(ZO):
        wz.append(send(buf_y.at[z], buf_y.at[z], s_wz.at[i], r_wz.at[z], z_dev(dz)))

    total = pr[:, pl.ds(pl.multiple_of(me_p * PR_ROWS, PR_ROWS), PR_ROWS), 0:XL]
    for copy in qcopies:
        copy.wait_recv()
    for n in range(len(XY)):
        total = total + buf_q[n]
    pq[...] = total
    zc = []
    for i, dz in enumerate(ORD):
        if dz:
            zc.append(send(pq.at[i], buf_z.at[i], s_qz.at[i], r_qz.at[i], z_dev(dz)))

    total = zs[pl.ds(pl.multiple_of(me_p * PR_ROWS, PR_ROWS), PR_ROWS), :]
    for i, copy in enumerate(xz):
        copy.wait_recv()
        total = total + buf_xz[i]
    fg[c, me_p, :, XL:KP] = total
    total = pq[NZ - 1]
    for i, copy in enumerate(zc):
        copy.wait_recv()
        total = total + buf_z[i]
    fg[c, me_p, :, 0:XL] = total
    qg = []
    for i, (dx, dy) in enumerate(XY):
        qg.append(
            send(fg.at[c, me_p], fg.at[c, me_p], s_qg.at[i], r_qg.at[me_p], plane_dev(plane(dx, dy)))
        )

    for dz in ZO:
        wz_recv(dz).wait_recv()
    total = buf_y[0]
    for k in range(1, NZ):
        total = total + buf_y[k]
    mine = pl.ds(pl.multiple_of(c * GH + me_p * GR, GR), GR)
    fw[mine, :] = total
    wg = []
    for i, (dx, dy) in enumerate(XY):
        wg.append(
            send(fw.at[mine], fw.at[mine], s_wg.at[i], r_wg.at[me_p], plane_dev(plane(dx, dy)))
        )

    for dx, dy in XY:
        p = plane(dx, dy)
        arrival(fg.at[c, p], s_qg.at[0], r_qg.at[p]).wait_recv()
    qc = send(fg.at[c], fg.at[c], s_qc, r_qc, sibling)
    qc.wait_recv()
    for dx, dy in XY:
        p = plane(dx, dy)
        arrival(fw.at[pl.ds(pl.multiple_of(c * GH + p * GR, GR), GR)], s_wg.at[0], r_wg.at[p]).wait_recv()
    half = pl.ds(pl.multiple_of(c * GH, GH), GH)
    wc = send(fw.at[half], fw.at[half], s_wc, r_wc, sibling)
    wc.wait_recv()
    out_f = pltpu.make_async_copy(fg, gproto_out, s_in.at[0])
    out_w = pltpu.make_async_copy(fw, gweight_out, s_in.at[1])
    out_f.start()
    out_w.start()
    out_f.wait()
    out_w.wait()

    for copy in pending:
        copy.wait_send()


def finish(batch_rows, fg, fw, protos, gproto_out, gweight_out, loss_out):
    g = fg[...].reshape(D, KP).T[0:KS, :]
    own = protos[...]
    pinv = lax.rsqrt(jnp.sum(own * own, axis=-1, keepdims=True) + TINY)
    u = own * pinv
    along = jnp.sum(u * g, axis=-1, keepdims=True)
    gproto_out[...] = (g - u * along) * pinv
    gweight_out[...] = fw[...]
    loss_out[...] = fg[0, 0, 0:1, KP - 1 : KP] * (-1.0 / (2.0 * batch_rows))


def body(features, projection, prototypes):
    rows = features.shape[0]
    batch_rows = rows * lax.axis_size("dp")
    dma = pltpu.SemaphoreType.DMA
    nxy, nz = len(XY), len(ZO)
    vm = pltpu.VMEM
    scratch = [
        vm((WR, 2, E), BF), vm((2, WR, E), BF), vm((E, D), BF), vm((KS, D), F32), dma((3,)),
        vm((KP, D), F32), vm((NZ, KP, D), BF), vm((2 * WR, D), F32), vm((2 * WR, 1), F32),
        vm((3 * WR, D), BF), vm((D, 2 * WR), BF), vm((E, 2 * WR), BF),
        vm((NZ, 3 * WR, KP), F32), vm((NZ, 2 * WR, KP), F32), vm((NZ, 2 * WR, KP), F32),
        vm((2 * WR, 1), F32), vm((NZ, 8, KP), F32), vm((3, NT, 128), F32), vm((3, NT, 128), F32),
        vm((NT, 128), F32), vm((NZ, 2 * WR, KP), BF),
        vm((3, nxy, NT, 128), F32), vm((3, nz, NT, 128), F32), vm((3, NT, 128), F32),
        vm((2 * WR, D), F32), vm((NZ, D, KP), F32), vm((NZ, RH, KP), F32), vm((NZ, RH, KP), F32),
        vm((nxy, NZ, PR_ROWS, XL), F32), vm((NZ, PR_ROWS, XL), F32), vm((nz, PR_ROWS, XL), F32),
        vm((NZ, RH, KP - XL), F32), vm((RH, KP - XL), F32), vm((nxy, PR_ROWS, KP - XL), F32),
        vm((NC, NP, PR_ROWS, KP), F32), vm((E, D), F32), vm((GH, D), F32),
        vm((GH, D), F32), vm((nxy, GR, D), F32), vm((NZ, GR, D), F32), vm((E, D), F32),
        vm((8, 128), F32),
        dma((nz,)), dma((nz,)), dma((nz,)), dma((nz,)), dma, dma,
        dma((3, nxy)), dma((3, nxy)), dma((3, nz)), dma((3, nz)), dma, dma,
        dma((NZ,)), dma((NZ,)), dma((NZ // GRPS, nxy)), dma((NZ // GRPS, nxy)), dma((NZ,)), dma((NZ,)),
        dma((nxy,)), dma((nxy,)), dma((nz,)), dma((nz,)), dma((nxy,)), dma((NP,)), dma, dma,
        dma, dma, dma((nxy,)), dma((nxy,)), dma((nz,)), dma((NZ,)), dma((nxy,)), dma((NP,)), dma, dma,
    ]
    vspec = pl.BlockSpec(memory_space=pltpu.VMEM)
    aspec = pl.BlockSpec(memory_space=pl.ANY)
    fg, fw = pl.pallas_call(
        functools.partial(kernel, batch_rows),
        out_shape=(
            jax.ShapeDtypeStruct((NC, NP, PR_ROWS, KP), F32),
            jax.ShapeDtypeStruct((E, D), F32),
        ),
        in_specs=[aspec] * 3,
        out_specs=(aspec,) * 2,
        scratch_shapes=scratch,
        compiler_params=pltpu.CompilerParams(
            collective_id=0, has_side_effects=True, vmem_limit_bytes=VLIM * 1024 * 1024
        ),
        name="swav",
    )(features, projection, prototypes)
    gproto, gweight, loss = pl.pallas_call(
        functools.partial(finish, batch_rows),
        out_shape=(
            jax.ShapeDtypeStruct((KS, D), F32),
            jax.ShapeDtypeStruct((E, D), F32),
            jax.ShapeDtypeStruct((1, 1), F32),
        ),
        in_specs=[vspec] * 3,
        out_specs=(vspec,) * 3,
        name="finish",
    )(fg, fw, prototypes)
    return gproto, gweight, loss.reshape(())


def solution(mesh):
    return jax.shard_map(
        body,
        mesh=mesh,
        in_specs=(P("dp", None, None), P(), P("mp", None)),
        out_specs=(P("mp", None), P(), P()),
        check_vma=False,
    )
```

```python
import functools

import jax
import jax.numpy as jnp
from jax import lax
from jax.experimental import pallas as pl
from jax.experimental.pallas import tpu as pltpu
from jax.sharding import PartitionSpec as P

MESH = pl.DeviceIdType.MESH
BF = jnp.bfloat16
F32 = jnp.float32

EPSILON_CODES = 0.05
SOFTMAX_TEMPER = 0.1
LOSS_FACTOR = 4096.0
VLIM = 60
TINY = 1e-06

NX, NY, NC, NZ = 4, 4, 2, 8
NP = NX * NY
KS = 375
KP = 384
LT = KP // 128
NT = NZ * LT
WR = 256
D = 256
E = 512
HALF = KP // 2
DH = D // 2
PR_ROWS = KP // NP
GH = E // 2
GR = GH // NP
XY = [(dx, dy) for dx in range(NX) for dy in range(NY) if dx or dy]
ZO = [1, 7, 2, 6, 3, 5, 4]


def nt_dot(a, b):
    return lax.dot_general(a, b, (((1,), (1,)), ((), ())), preferred_element_type=F32)


def dot(a, b):
    return jnp.dot(a, b, preferred_element_type=F32)


def kernel(
    batch_rows,
    feats_in, weight_in, protos_in,
    gproto_out, gweight_out,
    raw, feats, weight, protos, s_in,
    pu, ph, unit, inv, emb, emb_line, xt,
    ex, sc, so, so_line, den, rsc, acc, vec, csum, cothers, gm,
    buf_a, buf_b, vec_b,
    eg, gm_line, col, lanes, share_z, pg, buf_p, pr, buf_q, fg, gw, buf_w, gwr, buf_x, buf_y, fw, loss_acc,
    s_z, r_z, s_f, r_f, s_e, r_e, s_a, r_a, s_b, r_b, s_c, r_c,
    s_l, r_l, s_v, r_v, s_h, r_h, s_p, r_p, s_q, r_q, s_qg, r_qg, s_qc, r_qc,
    s_w, r_w, s_wx, r_wx, s_wz, r_wz, s_wg, r_wg, s_wc, r_wc,
):
    dp = lax.axis_index("dp")
    z = lax.axis_index("mp")
    x, y, c = dp // (NY * NC), (dp // NC) % NY, dp % NC
    o = 1 - c
    me_p = x * NY + y
    gf = LOSS_FACTOR / (2.0 * batch_rows * SOFTMAX_TEMPER)
    pending = []

    def plane(dx, dy):
        px, py = (x + dx) % NX, (y + dy) % NY
        return px * NY + py

    def plane_dev(p):
        return {"dp": p * NC + c, "mp": z}

    def z_dev(dz):
        return {"dp": dp, "mp": (z + dz) % NZ}

    sibling = {"dp": dp + 1 - 2 * c, "mp": z}

    def send(src, dst, ssem, rsem, device):
        copy = pltpu.make_async_remote_copy(
            src_ref=src, dst_ref=dst, send_sem=ssem, recv_sem=rsem, device_id=device, device_id_type=MESH
        )
        copy.start()
        pending.append(copy)
        return copy

    def arrival(dst, ssem, rsem):
        return pltpu.make_async_remote_copy(
            src_ref=dst, dst_ref=dst, send_sem=ssem, recv_sem=rsem, device_id=sibling, device_id_type=MESH
        )

    def wz_recv(dz):
        k = (z + dz) % NZ
        return arrival(buf_y.at[k], s_wz.at[0], r_wz.at[k])

    barrier = pltpu.get_barrier_semaphore()
    pl.semaphore_signal(barrier, inc=1, device_id=sibling, device_id_type=MESH)
    for dx, dy in XY:
        pl.semaphore_signal(barrier, inc=1, device_id=plane_dev(plane(dx, dy)), device_id_type=MESH)
    for dz in ZO:
        pl.semaphore_signal(barrier, inc=1, device_id=z_dev(dz), device_id_type=MESH)

    loads = [
        pltpu.make_async_copy(protos_in, protos, s_in.at[0]),
        pltpu.make_async_copy(feats_in.at[pl.ds(z * WR, WR)], raw, s_in.at[1]),
        pltpu.make_async_copy(weight_in, weight, s_in.at[2]),
    ]
    for load in loads:
        load.start()

    loads[0].wait()
    pu[...] = jnp.zeros_like(pu)
    own = protos[...]
    pu[0:KS, :] = own * lax.rsqrt(jnp.sum(own * own, axis=-1, keepdims=True) + TINY)
    ph[z] = pu[...].astype(BF)
    pl.semaphore_wait(barrier, 1 + len(XY) + len(ZO))

    zcopies = {}
    for i, dz in enumerate(ZO):
        part = ph.at[z, pl.ds(pl.multiple_of(c * HALF, HALF), HALF)]
        zcopies[dz] = send(part, part, s_z.at[i], r_z.at[i], z_dev(dz))

    loads[1].wait()
    loads[2].wait()
    to = lax.broadcasted_iota(jnp.int32, (2 * WR, 2 * WR), 0)
    fro = lax.broadcasted_iota(jnp.int32, (2 * WR, 2 * WR), 1)
    order = ((to % WR) * 2 + to // WR == fro).astype(F32).astype(BF)
    feats[...] = dot(order, raw[...].reshape(2 * WR, E)).astype(BF).reshape(2, WR, E)

    def embed(view, row, erow):
        raw = dot(feats[view], weight[...])
        inverse = lax.rsqrt(jnp.sum(raw * raw, axis=-1, keepdims=True) + TINY)
        u = raw * inverse
        inv[row : row + WR, :] = inverse
        unit[row : row + WR, :] = u
        emb[erow : erow + WR, :] = u.astype(BF)

    embed(o, WR, 2 * WR)
    ecopy = send(emb.at[pl.ds(2 * WR, WR)], emb.at[pl.ds(WR, WR)], s_e, r_e, sibling)
    embed(c, 0, 0)
    ecopy.wait_recv()

    def scores_slab(q):
        pq_ = ph[q]
        tot = jnp.zeros((8, KP), F32)
        for b in range(2):
            s = nt_dot(emb[b * WR : (b + 1) * WR, :], pq_)
            e = jnp.exp(s * (1.0 / EPSILON_CODES))
            ex[q, b * WR : (b + 1) * WR, :] = e
            if b == 0:
                sc[q, 0:WR, :] = s
            tot = tot + jnp.sum(e.reshape(WR // 8, 8, KP), axis=0)
        acc[q] = tot

    scores_slab(z)
    for i, dz in enumerate(ZO):
        q = (z + NZ - dz) % NZ
        zcopies[dz].wait_recv()
        part = ph.at[q, pl.ds(pl.multiple_of(c * HALF, HALF), HALF)]
        fwd = send(part, part, s_f.at[i], r_f.at[i], sibling)
        fwd.wait_recv()
        scores_slab(q)

    lane = lax.broadcasted_iota(jnp.int32, (NT, 128), 1)
    row = lax.broadcasted_iota(jnp.int32, (NT, 128), 0)
    valid = lane + (row % LT) * 128 < KS

    def finish_column_sums(k):
        for q in range(NZ):
            part = jnp.sum(acc[q], axis=0, keepdims=True)
            for j in range(LT):
                vec[k, q * LT + j : q * LT + j + 1, :] = part[:, j * 128 : (j + 1) * 128]

    def reduce_columns(k, work_a, work_b):
        finish_column_sums(k)
        copies = []
        for i, (dx, dy) in enumerate(XY):
            copies.append(
                send(vec.at[k], buf_a.at[k, i], s_a.at[k, i], r_a.at[k, i], plane_dev(plane(dx, dy)))
            )
        work_a()
        total = vec[k]
        for i, copy in enumerate(copies):
            copy.wait_recv()
            total = total + buf_a[k, i]
        vec_b[k] = total
        copies = []
        for i, dz in enumerate(ZO):
            copies.append(send(vec_b.at[k], buf_b.at[k, i], s_b.at[k, i], r_b.at[k, i], z_dev(dz)))
        work_b()
        for i, copy in enumerate(copies):
            copy.wait_recv()
            total = total + buf_b[k, i]
        csum[k] = jnp.where(valid, 1.0 / total, 0.0)

    def other_view():
        def step(q, carry):
            s = nt_dot(emb[2 * WR : 3 * WR, :], ph[q])
            ex[q, 2 * WR : 3 * WR, :] = jnp.exp(s * (1.0 / EPSILON_CODES))
            sc[q, WR : 2 * WR, :] = s
            return carry

        lax.fori_loop(0, NZ, step, 0)

    last = lax.broadcasted_iota(jnp.int32, (1, 128), 1) < KS - (LT - 1) * 128

    def denominators(first):
        R = 64

        def step(b, carry):
            rows = pl.ds(pl.multiple_of(first + b * R, R), R)
            total = jnp.zeros((R, 128), F32)
            for q in range(NZ):
                s = jnp.exp(sc[q, rows, :] * (1.0 / SOFTMAX_TEMPER))
                so[q, rows, :] = s
                for j in range(LT):
                    part = s[:, j * 128 : (j + 1) * 128]
                    if j == LT - 1:
                        part = jnp.where(last, part, 0.0)
                    total = total + part
            den[rows, :] = jnp.sum(total, axis=1, keepdims=True)
            return carry

        lax.fori_loop(0, WR // R, step, 0)

    def line_slot(dz):
        return (z + NZ + dz) % NZ

    def line_step(n):
        for i, way in enumerate((1, -1)):
            slot = line_slot(-way * (n - 1))
            part = emb_line.at[slot]
            if n == NZ // 2:
                part = emb_line.at[slot, pl.ds(i * WR, WR)]
            send(part, part, s_l.at[n - 1, i], r_l.at[n - 1, i], z_dev(way % NZ))

    def line_wait(n):
        for i, way in enumerate((1, -1)):
            slot = line_slot(-way * n)
            part = emb_line.at[slot]
            if n == NZ // 2:
                part = emb_line.at[slot, pl.ds(i * WR, WR)]
            arrival(part, s_l.at[n - 1, i], r_l.at[n - 1, i]).wait_recv()

    def line_scores(dz):
        slot = line_slot(dz)
        s = nt_dot(ph[z], emb_line[slot])
        so_line[slot] = jnp.exp(s * (1.0 / SOFTMAX_TEMPER))

    eye = lax.broadcasted_iota(jnp.int32, (128, 128), 0) == lax.broadcasted_iota(jnp.int32, (128, 128), 1)

    def to_lanes(ref, row):
        for i in range(2 * WR // 128):
            part = jnp.broadcast_to(ref[i * 128 : (i + 1) * 128, :], (128, 128))
            lanes[z, row + i : row + i + 1, :] = jnp.sum(jnp.where(eye, part, 0.0), axis=0, keepdims=True)

    def transposes_x():
        xt[:, 0:WR] = feats[c].astype(F32).T.astype(BF)
        xt[:, WR : 2 * WR] = feats[o].astype(F32).T.astype(BF)

    def row_inverse(cs, rows, R):
        total = jnp.zeros((R, 128), F32)
        for q in range(NZ):
            for j in range(LT):
                t = q * LT + j
                total = total + ex[q, rows, j * 128 : (j + 1) * 128] * cs[t : t + 1, :]
        return 1.0 / jnp.sum(total, axis=1, keepdims=True)

    def sinkhorn_pass(k):
        R = 64
        acc[...] = jnp.zeros_like(acc)

        def step(b, carry):
            rows = pl.ds(pl.multiple_of(b * R, R), R)
            r = row_inverse(csum.at[k], rows, R)
            for q in range(NZ):
                t = ex[q, rows, :] * r
                acc[q] += jnp.sum(t.reshape(R // 8, 8, KP), axis=0)
            return carry

        lax.fori_loop(0, 2 * WR // R, step, 0)

    def nothing():
        pass

    emb_line[z, 0:WR, :] = emb[0:WR, :]
    emb_line[z, WR : 2 * WR, :] = emb[2 * WR : 3 * WR, :]

    def work_1a():
        line_step(1)
        other_view()
        line_scores(0)

    def work_2b():
        line_scores(-1)
        line_scores(1)
        to_lanes(den, 4)

    def work_3a():
        transposes_x()
        line_scores(-2)

    reduce_columns(0, work_1a, lambda: denominators(0))
    line_wait(1)
    line_step(2)
    sinkhorn_pass(0)
    reduce_columns(1, lambda: denominators(WR), work_2b)
    line_wait(2)
    line_step(3)
    sinkhorn_pass(1)
    reduce_columns(2, work_3a, lambda: line_scores(2))
    ccopy = send(csum.at[2], cothers, s_c, r_c, sibling)
    line_wait(3)
    line_step(4)

    def row_scales(cs, row, erow):
        def step(b, carry):
            R = 64
            rows = pl.ds(pl.multiple_of(row + b * R, R), R)
            rsc[rows, :] = row_inverse(cs, pl.ds(pl.multiple_of(erow + b * R, R), R), R)
            return carry

        lax.fori_loop(0, WR // 64, step, 0)

    row_scales(csum.at[2], 0, 0)
    ccopy.wait_recv()
    row_scales(cothers, WR, 2 * WR)
    to_lanes(rsc, 0)
    for i, dz in enumerate(ZO):
        send(lanes.at[z], lanes.at[z], s_v.at[i], r_v.at[z], z_dev(dz))
    line_scores(-3)
    line_scores(3)

    RG = 32
    loss_acc[...] = jnp.zeros_like(loss_acc)

    def grad_step(b, carry):
        rows_c = pl.ds(pl.multiple_of(b * RG, RG), RG)
        rows_o = pl.ds(pl.multiple_of(WR + b * RG, RG), RG)
        erows_o = pl.ds(pl.multiple_of(2 * WR + b * RG, RG), RG)
        rc = rsc[rows_c, :] * gf
        ro = rsc[rows_o, :] * gf
        dc = gf / den[rows_c, :]
        do = gf / den[rows_o, :]
        total = jnp.zeros((RG, 128), F32)
        for q in range(NZ):
            for j in range(LT):
                t = q * LT + j
                cols = slice(j * 128, (j + 1) * 128)
                ac = ex[q, rows_c, cols] * csum[2, t : t + 1, :] * rc
                ao = ex[q, erows_o, cols] * cothers[t : t + 1, :] * ro
                gm[q, rows_c, cols] = (so[q, rows_c, cols] * dc - ao).astype(BF)
                gm[q, rows_o, cols] = (so[q, rows_o, cols] * do - ac).astype(BF)
                total = total + ao * sc[q, rows_c, cols] + ac * sc[q, rows_o, cols]
        loss_acc[...] += jnp.sum(total.reshape(RG // 8, 8, 128), axis=0)
        return carry

    lax.fori_loop(0, WR // RG, grad_step, 0)

    log_total = jnp.sum(jnp.log(den[...]))
    share = jnp.sum(loss_acc[...]) * (1.0 / (SOFTMAX_TEMPER * gf)) - log_total
    share_z[z] = jnp.full((8, 128), share, F32)
    for i, dz in enumerate(ZO):
        send(share_z.at[z], share_z.at[z], s_h.at[i], r_h.at[z], z_dev(dz))

    grads = jnp.zeros((2 * WR, D), F32)
    for q in range(NZ):
        grads = grads + dot(gm[q], ph[q])
    eg[...] = grads
    along = jnp.sum(unit[...] * eg[...], axis=-1, keepdims=True)
    graw = ((eg[...] - unit[...] * along) * inv[...]).astype(BF)
    gw[...] = dot(xt[...], graw)
    wcopy = send(gw.at[pl.ds(pl.multiple_of(o * GH, GH), GH)], buf_w, s_w, r_w, sibling)
    wcopy.wait_recv()
    gwr[...] = gw[pl.ds(pl.multiple_of(c * GH, GH), GH), :] + buf_w[...]
    wcopies = []
    for i, (dx, dy) in enumerate(XY):
        p = plane(dx, dy)
        wcopies.append(
            send(gwr.at[pl.ds(pl.multiple_of(p * GR, GR), GR)], buf_x.at[i], s_wx.at[i], r_wx.at[i], plane_dev(p))
        )

    for v, cs in enumerate((csum.at[2], cothers)):
        for j in range(LT):
            part = jnp.broadcast_to(cs[pl.ds(z * LT + j, 1), :], (128, 128))
            part = jnp.sum(jnp.where(eye, part, 0.0), axis=1, keepdims=True)
            col[v, j * 128 : (j + 1) * 128, :] = jnp.broadcast_to(part, (128, 128))
    line_wait(4)
    line_scores(4)
    for dz in ZO:
        k = line_slot(dz)
        arrival(lanes.at[k], s_v.at[0], r_v.at[k]).wait_recv()

    def line_grad(k, carry):
        scale = [lanes[k, i : i + 1, :] * gf for i in range(4)]
        soft = [gf / lanes[k, i : i + 1, :] for i in range(4, 8)]
        R = 32
        for b in range(KP // R):
            rows = slice(b * R, (b + 1) * R)
            for i in range(2):
                lc, lo = slice(i * 128, (i + 1) * 128), slice(WR + i * 128, WR + (i + 1) * 128)
                sc_, so_ = so_line[k, rows, lc], so_line[k, rows, lo]
                ac = sc_ * sc_ * col[0, rows, :] * scale[i]
                ao = so_ * so_ * col[1, rows, :] * scale[2 + i]
                gm_line[k, rows, lc] = (sc_ * soft[i] - ao).astype(BF)
                gm_line[k, rows, lo] = (so_ * soft[2 + i] - ac).astype(BF)
        return carry

    lax.fori_loop(0, NZ, line_grad, 0)
    grads = jnp.zeros((KP, D), F32)
    for k in range(NZ):
        grads = grads + dot(gm_line[k], emb_line[k])
    pg[...] = grads
    for dz in ZO:
        k = line_slot(dz)
        arrival(share_z.at[k], s_h.at[0], r_h.at[k]).wait_recv()
    share = share_z[0, 0:1, 0:1]
    for k in range(1, NZ):
        share = share + share_z[k, 0:1, 0:1]
    spare = lax.broadcasted_iota(jnp.int32, (8, D), 0) == 7
    pg[KP - 8 : KP, :] = jnp.where(spare, share, pg[KP - 8 : KP, :])
    pcopy = send(pg.at[:, pl.ds(pl.multiple_of(o * DH, DH), DH)], buf_p, s_p, r_p, sibling)
    pcopy.wait_recv()
    pr[...] = pg[:, pl.ds(pl.multiple_of(c * DH, DH), DH)] + buf_p[...]
    qcopies = []
    for i, (dx, dy) in enumerate(XY):
        p = plane(dx, dy)
        qcopies.append(
            send(pr.at[pl.ds(pl.multiple_of(p * PR_ROWS, PR_ROWS), PR_ROWS)], buf_q.at[i], s_q.at[i], r_q.at[i], plane_dev(p))
        )

    total = gwr[pl.ds(pl.multiple_of(me_p * GR, GR), GR), :]
    for i, copy in enumerate(wcopies):
        copy.wait_recv()
        total = total + buf_x[i]
    buf_y[z] = total
    wz = []
    for i, dz in enumerate(ZO):
        wz.append(send(buf_y.at[z], buf_y.at[z], s_wz.at[i], r_wz.at[z], z_dev(dz)))

    mine = pl.ds(pl.multiple_of(me_p * PR_ROWS, PR_ROWS), PR_ROWS)
    total = pr[mine, :]
    for i, copy in enumerate(qcopies):
        copy.wait_recv()
        total = total + buf_q[i]
    fg[c, mine, :] = total
    for i, (dx, dy) in enumerate(XY):
        send(fg.at[c, mine], fg.at[c, mine], s_qg.at[i], r_qg.at[me_p], plane_dev(plane(dx, dy)))

    for dz in ZO:
        wz_recv(dz).wait_recv()
    total = buf_y[0]
    for k in range(1, NZ):
        total = total + buf_y[k]
    mine = pl.ds(pl.multiple_of(c * GH + me_p * GR, GR), GR)
    fw[mine, :] = total
    wg = []
    for i, (dx, dy) in enumerate(XY):
        wg.append(
            send(fw.at[mine], fw.at[mine], s_wg.at[i], r_wg.at[me_p], plane_dev(plane(dx, dy)))
        )

    for dx, dy in XY:
        p = plane(dx, dy)
        part = pl.ds(pl.multiple_of(p * PR_ROWS, PR_ROWS), PR_ROWS)
        arrival(fg.at[c, part], s_qg.at[0], r_qg.at[p]).wait_recv()
    qc = send(fg.at[c], fg.at[c], s_qc, r_qc, sibling)
    qc.wait_recv()
    for dx, dy in XY:
        p = plane(dx, dy)
        arrival(fw.at[pl.ds(pl.multiple_of(c * GH + p * GR, GR), GR)], s_wg.at[0], r_wg.at[p]).wait_recv()
    half = pl.ds(pl.multiple_of(c * GH, GH), GH)
    wc = send(fw.at[half], fw.at[half], s_wc, r_wc, sibling)
    wc.wait_recv()
    out_f = pltpu.make_async_copy(fg, gproto_out, s_in.at[0])
    out_w = pltpu.make_async_copy(fw, gweight_out, s_in.at[1])
    out_f.start()
    out_w.start()
    out_f.wait()
    out_w.wait()

    for copy in pending:
        copy.wait_send()


def finish(batch_rows, fg, fw, protos, gproto_out, gweight_out, loss_out):
    g = jnp.concatenate([fg[0], fg[1]], axis=1)[0:KS, :]
    own = protos[...]
    pinv = lax.rsqrt(jnp.sum(own * own, axis=-1, keepdims=True) + TINY)
    u = own * pinv
    along = jnp.sum(u * g, axis=-1, keepdims=True)
    gproto_out[...] = (g - u * along) * pinv
    gweight_out[...] = fw[...]
    loss_out[...] = fg[0, KP - 1 : KP, 0:1] * (-1.0 / (2.0 * batch_rows))


def body(features, projection, prototypes):
    rows = features.shape[0]
    batch_rows = rows * lax.axis_size("dp")
    dma = pltpu.SemaphoreType.DMA
    nxy, nz = len(XY), len(ZO)
    vm = pltpu.VMEM
    scratch = [
        vm((WR, 2, E), BF), vm((2, WR, E), BF), vm((E, D), BF), vm((KS, D), F32), dma((3,)),
        vm((KP, D), F32), vm((NZ, KP, D), BF), vm((2 * WR, D), F32), vm((2 * WR, 1), F32),
        vm((3 * WR, D), BF), vm((NZ, 2 * WR, D), BF), vm((E, 2 * WR), BF),
        vm((NZ, 3 * WR, KP), F32), vm((NZ, 2 * WR, KP), F32), vm((NZ, 2 * WR, KP), F32), vm((NZ, KP, 2 * WR), F32),
        vm((2 * WR, 1), F32), vm((2 * WR, 1), F32), vm((NZ, 8, KP), F32), vm((3, NT, 128), F32), vm((3, NT, 128), F32),
        vm((NT, 128), F32), vm((NZ, 2 * WR, KP), BF),
        vm((3, nxy, NT, 128), F32), vm((3, nz, NT, 128), F32), vm((3, NT, 128), F32),
        vm((2 * WR, D), F32), vm((NZ, KP, 2 * WR), BF), vm((2, KP, 128), F32), vm((NZ, 8, 128), F32), vm((NZ, 8, 128), F32),
        vm((KP, D), F32), vm((KP, DH), F32), vm((KP, DH), F32), vm((nxy, PR_ROWS, DH), F32), vm((NC, KP, DH), F32),
        vm((E, D), F32), vm((GH, D), F32), vm((GH, D), F32), vm((nxy, GR, D), F32), vm((NZ, GR, D), F32), vm((E, D), F32),
        vm((8, 128), F32),
        dma((nz,)), dma((nz,)), dma((nz,)), dma((nz,)), dma, dma,
        dma((3, nxy)), dma((3, nxy)), dma((3, nz)), dma((3, nz)), dma, dma,
        dma((4, 2)), dma((4, 2)), dma((nz,)), dma((NZ,)), dma((nz,)), dma((NZ,)), dma, dma,
        dma((nxy,)), dma((nxy,)), dma((nxy,)), dma((NP,)), dma, dma,
        dma, dma, dma((nxy,)), dma((nxy,)), dma((nz,)), dma((NZ,)), dma((nxy,)), dma((NP,)), dma, dma,
    ]
    vspec = pl.BlockSpec(memory_space=pltpu.VMEM)
    aspec = pl.BlockSpec(memory_space=pl.ANY)
    fg, fw = pl.pallas_call(
        functools.partial(kernel, batch_rows),
        out_shape=(
            jax.ShapeDtypeStruct((NC, KP, DH), F32),
            jax.ShapeDtypeStruct((E, D), F32),
        ),
        in_specs=[aspec] * 3,
        out_specs=(aspec,) * 2,
        scratch_shapes=scratch,
        compiler_params=pltpu.CompilerParams(
            collective_id=0, has_side_effects=True, vmem_limit_bytes=VLIM * 1024 * 1024
        ),
        name="swav",
    )(features, projection, prototypes)
    gproto, gweight, loss = pl.pallas_call(
        functools.partial(finish, batch_rows),
        out_shape=(
            jax.ShapeDtypeStruct((KS, D), F32),
            jax.ShapeDtypeStruct((E, D), F32),
            jax.ShapeDtypeStruct((1, 1), F32),
        ),
        in_specs=[vspec] * 3,
        out_specs=(vspec,) * 3,
        name="finish",
    )(fg, fw, prototypes)
    return gproto, gweight, loss.reshape(())


def solution(mesh):
    return jax.shard_map(
        body,
        mesh=mesh,
        in_specs=(P("dp", None, None), P(), P("mp", None)),
        out_specs=(P("mp", None), P(), P()),
        check_vma=False,
    )
```

```python
import functools

import jax
import jax.numpy as jnp
from jax import lax
from jax.experimental import pallas as pl
from jax.experimental.pallas import tpu as pltpu
from jax.sharding import PartitionSpec as P

MESH = pl.DeviceIdType.MESH
BF = jnp.bfloat16
F32 = jnp.float32

EPSILON_CODES = 0.05
SOFTMAX_TEMPER = 0.1
LOSS_FACTOR = 4096.0
VLIM = 60
TINY = 1e-06

NX, NY, NC, NZ = 4, 4, 2, 8
NP = NX * NY
KS = 375
KP = 384
LT = KP // 128
NT = NZ * LT
WR = 256
D = 256
E = 512
NQ = 4
QR = KP // NQ // NC
DH = D // 2
PR_ROWS = KP // NP
GH = E // 2
GR = GH // NP
XY = [(dx, dy) for dx in range(NX) for dy in range(NY) if dx or dy]
ZO = [1, 7, 2, 6, 3, 5, 4]
FAR = [4, 3, 5, 2, 6]
NEAR = [1, 7]
NB = [(1, 0), (-1, 0), (0, 1)]


def nt_dot(a, b):
    return lax.dot_general(a, b, (((1,), (1,)), ((), ())), preferred_element_type=F32)


def dot(a, b):
    return jnp.dot(a, b, preferred_element_type=F32)


def kernel(
    batch_rows,
    feats_in, weight_in, protos_in,
    gproto_out, gweight_out,
    raw, feats, weight, protos, s_in,
    pu, ph, unit, inv, emb, emb_line, xt,
    ex, sc, so, so_line, den, rsc, acc, vec, csum, cothers, gm,
    buf_a, buf_b, vec_b,
    eg, gm_line, col, lanes, share_z, pg, buf_p, pr, buf_q, fg, gw, buf_w, gwr, buf_x, buf_y, fw, loss_acc,
    s_z, r_z, s_n, r_n, s_f, r_f, s_e, r_e, s_a, r_a, s_b, r_b, s_c, r_c,
    s_l, r_l, s_v, r_v, s_h, r_h, s_p, r_p, s_q, r_q, s_qg, r_qg, s_qc, r_qc,
    s_w, r_w, s_wx, r_wx, s_wz, r_wz, s_wg, r_wg, s_wc, r_wc,
):
    dp = lax.axis_index("dp")
    z = lax.axis_index("mp")
    x, y, c = dp // (NY * NC), (dp // NC) % NY, dp % NC
    o = 1 - c
    me_p = x * NY + y
    gf = LOSS_FACTOR / (2.0 * batch_rows * SOFTMAX_TEMPER)
    pending = []

    def plane(dx, dy):
        px, py = (x + dx) % NX, (y + dy) % NY
        return px * NY + py

    def plane_dev(p):
        return {"dp": p * NC + c, "mp": z}

    def z_dev(dz):
        return {"dp": dp, "mp": (z + dz) % NZ}

    sibling = {"dp": dp + 1 - 2 * c, "mp": z}

    def send(src, dst, ssem, rsem, device):
        copy = pltpu.make_async_remote_copy(
            src_ref=src, dst_ref=dst, send_sem=ssem, recv_sem=rsem, device_id=device, device_id_type=MESH
        )
        copy.start()
        pending.append(copy)
        return copy

    def arrival(dst, ssem, rsem):
        return pltpu.make_async_remote_copy(
            src_ref=dst, dst_ref=dst, send_sem=ssem, recv_sem=rsem, device_id=sibling, device_id_type=MESH
        )

    def wz_recv(dz):
        k = (z + dz) % NZ
        return arrival(buf_y.at[k], s_wz.at[0], r_wz.at[k])

    barrier = pltpu.get_barrier_semaphore()
    pl.semaphore_signal(barrier, inc=1, device_id=sibling, device_id_type=MESH)
    for dx, dy in XY:
        pl.semaphore_signal(barrier, inc=1, device_id=plane_dev(plane(dx, dy)), device_id_type=MESH)
    for dz in ZO:
        pl.semaphore_signal(barrier, inc=1, device_id=z_dev(dz), device_id_type=MESH)

    loads = [
        pltpu.make_async_copy(protos_in, protos, s_in.at[0]),
        pltpu.make_async_copy(feats_in.at[pl.ds(z * WR, WR)], raw, s_in.at[1]),
        pltpu.make_async_copy(weight_in, weight, s_in.at[2]),
    ]
    for load in loads:
        load.start()

    loads[0].wait()
    pu[...] = jnp.zeros_like(pu)
    own = protos[...]
    pu[0:KS, :] = own * lax.rsqrt(jnp.sum(own * own, axis=-1, keepdims=True) + TINY)
    ph[z] = pu[...].astype(BF).reshape(NQ, NC, QR, D)
    pl.semaphore_wait(barrier, 1 + len(XY) + len(ZO))

    colour = (x + 2 * y) % NQ
    for i, dz in enumerate(FAR):
        part = ph.at[z, colour, c]
        send(part, part, s_z.at[i], r_z.at[i], z_dev(dz))
    for i, dz in enumerate(NEAR):
        part = ph.at[z, :, c]
        send(part, part, s_z.at[len(FAR) + i], r_z.at[len(FAR) + i], z_dev(dz))

    def slab(q):
        return ph[q].reshape(KP, D)

    loads[1].wait()
    loads[2].wait()
    to = lax.broadcasted_iota(jnp.int32, (2 * WR, 2 * WR), 0)
    fro = lax.broadcasted_iota(jnp.int32, (2 * WR, 2 * WR), 1)
    order = ((to % WR) * 2 + to // WR == fro).astype(F32).astype(BF)
    feats[...] = dot(order, raw[...].reshape(2 * WR, E)).astype(BF).reshape(2, WR, E)

    def embed(view, row, erow):
        raw = dot(feats[view], weight[...])
        inverse = lax.rsqrt(jnp.sum(raw * raw, axis=-1, keepdims=True) + TINY)
        u = raw * inverse
        inv[row : row + WR, :] = inverse
        unit[row : row + WR, :] = u
        emb[erow : erow + WR, :] = u.astype(BF)

    embed(o, WR, 2 * WR)
    ecopy = send(emb.at[pl.ds(2 * WR, WR)], emb.at[pl.ds(WR, WR)], s_e, r_e, sibling)
    embed(c, 0, 0)
    ecopy.wait_recv()

    def scores_slab(q):
        pq_ = slab(q)
        tot = jnp.zeros((8, KP), F32)
        for b in range(2):
            s = nt_dot(emb[b * WR : (b + 1) * WR, :], pq_)
            e = jnp.exp(s * (1.0 / EPSILON_CODES))
            ex[q, b * WR : (b + 1) * WR, :] = e
            if b == 0:
                sc[q, 0:WR, :] = s
            tot = tot + jnp.sum(e.reshape(WR // 8, 8, KP), axis=0)
        acc[q] = tot

    scores_slab(z)
    came = [(z + NZ - dz) % NZ for dz in FAR + NEAR]
    for i in range(len(FAR)):
        part = ph.at[came[i], colour, c]
        arrival(part, s_z.at[i], r_z.at[i]).wait_recv()
        for n, (dx, dy) in enumerate(NB):
            send(part, part, s_n.at[i, n], r_n.at[i, n], plane_dev(plane(dx, dy)))

    def to_sibling(i):
        part = ph.at[came[i], :, c]
        return send(part, part, s_f.at[i], r_f.at[i], sibling)

    forwards = {}
    for i in (len(FAR), len(FAR) + 1):
        arrival(ph.at[came[i], :, c], s_z.at[i], r_z.at[i]).wait_recv()
        forwards[i] = to_sibling(i)
    for i in (len(FAR), len(FAR) + 1):
        forwards[i].wait_recv()
        scores_slab(came[i])
    for i in range(len(FAR) + 1):
        if i < len(FAR):
            for n, (dx, dy) in enumerate(NB):
                part = ph.at[came[i], (colour + 3 * NQ - dx - 2 * dy) % NQ, c]
                arrival(part, s_n.at[i, n], r_n.at[i, n]).wait_recv()
            forwards[i] = to_sibling(i)
        if i:
            forwards[i - 1].wait_recv()
            scores_slab(came[i - 1])

    lane = lax.broadcasted_iota(jnp.int32, (NT, 128), 1)
    row = lax.broadcasted_iota(jnp.int32, (NT, 128), 0)
    valid = lane + (row % LT) * 128 < KS

    def finish_column_sums(k):
        for q in range(NZ):
            part = jnp.sum(acc[q], axis=0, keepdims=True)
            for j in range(LT):
                vec[k, q * LT + j : q * LT + j + 1, :] = part[:, j * 128 : (j + 1) * 128]

    def reduce_columns(k, work_a, work_b):
        finish_column_sums(k)
        copies = []
        for i, (dx, dy) in enumerate(XY):
            copies.append(
                send(vec.at[k], buf_a.at[k, i], s_a.at[k, i], r_a.at[k, i], plane_dev(plane(dx, dy)))
            )
        work_a()
        total = vec[k]
        for i, copy in enumerate(copies):
            copy.wait_recv()
            total = total + buf_a[k, i]
        vec_b[k] = total
        copies = []
        for i, dz in enumerate(ZO):
            copies.append(send(vec_b.at[k], buf_b.at[k, i], s_b.at[k, i], r_b.at[k, i], z_dev(dz)))
        work_b()
        for i, copy in enumerate(copies):
            copy.wait_recv()
            total = total + buf_b[k, i]
        csum[k] = jnp.where(valid, 1.0 / total, 0.0)

    def other_view():
        def step(q, carry):
            s = nt_dot(emb[2 * WR : 3 * WR, :], slab(q))
            ex[q, 2 * WR : 3 * WR, :] = jnp.exp(s * (1.0 / EPSILON_CODES))
            sc[q, WR : 2 * WR, :] = s
            return carry

        lax.fori_loop(0, NZ, step, 0)

    last = lax.broadcasted_iota(jnp.int32, (1, 128), 1) < KS - (LT - 1) * 128

    def denominators(first):
        R = 64

        def step(b, carry):
            rows = pl.ds(pl.multiple_of(first + b * R, R), R)
            total = jnp.zeros((R, 128), F32)
            for q in range(NZ):
                s = jnp.exp(sc[q, rows, :] * (1.0 / SOFTMAX_TEMPER))
                so[q, rows, :] = s
                for j in range(LT):
                    part = s[:, j * 128 : (j + 1) * 128]
                    if j == LT - 1:
                        part = jnp.where(last, part, 0.0)
                    total = total + part
            den[rows, :] = jnp.sum(total, axis=1, keepdims=True)
            return carry

        lax.fori_loop(0, WR // R, step, 0)

    def line_slot(dz):
        return (z + NZ + dz) % NZ

    def line_step(n):
        for i, way in enumerate((1, -1)):
            slot = line_slot(-way * (n - 1))
            part = emb_line.at[slot]
            if n == NZ // 2:
                part = emb_line.at[slot, pl.ds(i * WR, WR)]
            send(part, part, s_l.at[n - 1, i], r_l.at[n - 1, i], z_dev(way % NZ))

    def line_wait(n):
        for i, way in enumerate((1, -1)):
            slot = line_slot(-way * n)
            part = emb_line.at[slot]
            if n == NZ // 2:
                part = emb_line.at[slot, pl.ds(i * WR, WR)]
            arrival(part, s_l.at[n - 1, i], r_l.at[n - 1, i]).wait_recv()

    def line_scores(dz):
        slot = line_slot(dz)
        s = nt_dot(slab(z), emb_line[slot])
        so_line[slot] = jnp.exp(s * (1.0 / SOFTMAX_TEMPER))

    eye = lax.broadcasted_iota(jnp.int32, (128, 128), 0) == lax.broadcasted_iota(jnp.int32, (128, 128), 1)

    def to_lanes(ref, row):
        for i in range(2 * WR // 128):
            part = jnp.broadcast_to(ref[i * 128 : (i + 1) * 128, :], (128, 128))
            lanes[z, row + i : row + i + 1, :] = jnp.sum(jnp.where(eye, part, 0.0), axis=0, keepdims=True)

    def transposes_x():
        xt[:, 0:WR] = feats[c].astype(F32).T.astype(BF)
        xt[:, WR : 2 * WR] = feats[o].astype(F32).T.astype(BF)

    def row_inverse(cs, rows, R):
        total = jnp.zeros((R, 128), F32)
        for q in range(NZ):
            for j in range(LT):
                t = q * LT + j
                total = total + ex[q, rows, j * 128 : (j + 1) * 128] * cs[t : t + 1, :]
        return 1.0 / jnp.sum(total, axis=1, keepdims=True)

    def sinkhorn_pass(k):
        R = 64
        acc[...] = jnp.zeros_like(acc)

        def step(b, carry):
            rows = pl.ds(pl.multiple_of(b * R, R), R)
            r = row_inverse(csum.at[k], rows, R)
            for q in range(NZ):
                t = ex[q, rows, :] * r
                acc[q] += jnp.sum(t.reshape(R // 8, 8, KP), axis=0)
            return carry

        lax.fori_loop(0, 2 * WR // R, step, 0)

    def nothing():
        pass

    emb_line[z, 0:WR, :] = emb[0:WR, :]
    emb_line[z, WR : 2 * WR, :] = emb[2 * WR : 3 * WR, :]

    def work_1a():
        line_step(1)
        other_view()
        line_scores(0)

    def work_2b():
        line_scores(-1)
        line_scores(1)
        to_lanes(den, 4)

    def work_3a():
        transposes_x()
        line_scores(-2)

    reduce_columns(0, work_1a, lambda: denominators(0))
    line_wait(1)
    line_step(2)
    sinkhorn_pass(0)
    reduce_columns(1, lambda: denominators(WR), work_2b)
    line_wait(2)
    line_step(3)
    sinkhorn_pass(1)
    reduce_columns(2, work_3a, lambda: line_scores(2))
    ccopy = send(csum.at[2], cothers, s_c, r_c, sibling)
    line_wait(3)
    line_step(4)

    def row_scales(cs, row, erow):
        def step(b, carry):
            R = 64
            rows = pl.ds(pl.multiple_of(row + b * R, R), R)
            rsc[rows, :] = row_inverse(cs, pl.ds(pl.multiple_of(erow + b * R, R), R), R)
            return carry

        lax.fori_loop(0, WR // 64, step, 0)

    row_scales(csum.at[2], 0, 0)
    ccopy.wait_recv()
    row_scales(cothers, WR, 2 * WR)
    to_lanes(rsc, 0)
    for i, dz in enumerate(ZO):
        send(lanes.at[z], lanes.at[z], s_v.at[i], r_v.at[z], z_dev(dz))
    line_scores(-3)
    line_scores(3)

    RG = 32
    loss_acc[...] = jnp.zeros_like(loss_acc)

    def grad_step(b, carry):
        rows_c = pl.ds(pl.multiple_of(b * RG, RG), RG)
        rows_o = pl.ds(pl.multiple_of(WR + b * RG, RG), RG)
        erows_o = pl.ds(pl.multiple_of(2 * WR + b * RG, RG), RG)
        rc = rsc[rows_c, :] * gf
        ro = rsc[rows_o, :] * gf
        dc = gf / den[rows_c, :]
        do = gf / den[rows_o, :]
        total = jnp.zeros((RG, 128), F32)
        for q in range(NZ):
            for j in range(LT):
                t = q * LT + j
                cols = slice(j * 128, (j + 1) * 128)
                ac = ex[q, rows_c, cols] * csum[2, t : t + 1, :] * rc
                ao = ex[q, erows_o, cols] * cothers[t : t + 1, :] * ro
                gm[q, rows_c, cols] = (so[q, rows_c, cols] * dc - ao).astype(BF)
                gm[q, rows_o, cols] = (so[q, rows_o, cols] * do - ac).astype(BF)
                total = total + ao * sc[q, rows_c, cols] + ac * sc[q, rows_o, cols]
        loss_acc[...] += jnp.sum(total.reshape(RG // 8, 8, 128), axis=0)
        return carry

    lax.fori_loop(0, WR // RG, grad_step, 0)

    log_total = jnp.sum(jnp.log(den[...]))
    share = jnp.sum(loss_acc[...]) * (1.0 / (SOFTMAX_TEMPER * gf)) - log_total
    share_z[z] = jnp.full((8, 128), share, F32)
    for i, dz in enumerate(ZO):
        send(share_z.at[z], share_z.at[z], s_h.at[i], r_h.at[z], z_dev(dz))

    grads = jnp.zeros((2 * WR, D), F32)
    for q in range(NZ):
        grads = grads + dot(gm[q], slab(q))
    eg[...] = grads
    along = jnp.sum(unit[...] * eg[...], axis=-1, keepdims=True)
    graw = ((eg[...] - unit[...] * along) * inv[...]).astype(BF)
    gw[...] = dot(xt[...], graw)
    wcopy = send(gw.at[pl.ds(pl.multiple_of(o * GH, GH), GH)], buf_w, s_w, r_w, sibling)
    wcopy.wait_recv()
    gwr[...] = gw[pl.ds(pl.multiple_of(c * GH, GH), GH), :] + buf_w[...]
    wcopies = []
    for i, (dx, dy) in enumerate(XY):
        p = plane(dx, dy)
        wcopies.append(
            send(gwr.at[pl.ds(pl.multiple_of(p * GR, GR), GR)], buf_x.at[i], s_wx.at[i], r_wx.at[i], plane_dev(p))
        )

    for v, cs in enumerate((csum.at[2], cothers)):
        for j in range(LT):
            part = jnp.broadcast_to(cs[pl.ds(z * LT + j, 1), :], (128, 128))
            part = jnp.sum(jnp.where(eye, part, 0.0), axis=1, keepdims=True)
            col[v, j * 128 : (j + 1) * 128, :] = jnp.broadcast_to(part, (128, 128))
    line_wait(4)
    line_scores(4)
    for dz in ZO:
        k = line_slot(dz)
        arrival(lanes.at[k], s_v.at[0], r_v.at[k]).wait_recv()

    def line_grad(k, carry):
        scale = [lanes[k, i : i + 1, :] * gf for i in range(4)]
        soft = [gf / lanes[k, i : i + 1, :] for i in range(4, 8)]
        R = 32
        for b in range(KP // R):
            rows = slice(b * R, (b + 1) * R)
            for i in range(2):
                lc, lo = slice(i * 128, (i + 1) * 128), slice(WR + i * 128, WR + (i + 1) * 128)
                sc_, so_ = so_line[k, rows, lc], so_line[k, rows, lo]
                ac = sc_ * sc_ * col[0, rows, :] * scale[i]
                ao = so_ * so_ * col[1, rows, :] * scale[2 + i]
                gm_line[k, rows, lc] = (sc_ * soft[i] - ao).astype(BF)
                gm_line[k, rows, lo] = (so_ * soft[2 + i] - ac).astype(BF)
        return carry

    lax.fori_loop(0, NZ, line_grad, 0)
    grads = jnp.zeros((KP, D), F32)
    for k in range(NZ):
        grads = grads + dot(gm_line[k], emb_line[k])
    pg[...] = grads
    for dz in ZO:
        k = line_slot(dz)
        arrival(share_z.at[k], s_h.at[0], r_h.at[k]).wait_recv()
    share = share_z[0, 0:1, 0:1]
    for k in range(1, NZ):
        share = share + share_z[k, 0:1, 0:1]
    spare = lax.broadcasted_iota(jnp.int32, (8, D), 0) == 7
    pg[KP - 8 : KP, :] = jnp.where(spare, share, pg[KP - 8 : KP, :])
    pcopy = send(pg.at[:, pl.ds(pl.multiple_of(o * DH, DH), DH)], buf_p, s_p, r_p, sibling)
    pcopy.wait_recv()
    pr[...] = pg[:, pl.ds(pl.multiple_of(c * DH, DH), DH)] + buf_p[...]
    qcopies = []
    for i, (dx, dy) in enumerate(XY):
        p = plane(dx, dy)
        qcopies.append(
            send(pr.at[pl.ds(pl.multiple_of(p * PR_ROWS, PR_ROWS), PR_ROWS)], buf_q.at[i], s_q.at[i], r_q.at[i], plane_dev(p))
        )

    total = gwr[pl.ds(pl.multiple_of(me_p * GR, GR), GR), :]
    for i, copy in enumerate(wcopies):
        copy.wait_recv()
        total = total + buf_x[i]
    buf_y[z] = total
    wz = []
    for i, dz in enumerate(ZO):
        wz.append(send(buf_y.at[z], buf_y.at[z], s_wz.at[i], r_wz.at[z], z_dev(dz)))

    mine = pl.ds(pl.multiple_of(me_p * PR_ROWS, PR_ROWS), PR_ROWS)
    total = pr[mine, :]
    for i, copy in enumerate(qcopies):
        copy.wait_recv()
        total = total + buf_q[i]
    fg[c, mine, :] = total
    for i, (dx, dy) in enumerate(XY):
        send(fg.at[c, mine], fg.at[c, mine], s_qg.at[i], r_qg.at[me_p], plane_dev(plane(dx, dy)))

    for dz in ZO:
        wz_recv(dz).wait_recv()
    total = buf_y[0]
    for k in range(1, NZ):
        total = total + buf_y[k]
    mine = pl.ds(pl.multiple_of(c * GH + me_p * GR, GR), GR)
    fw[mine, :] = total
    wg = []
    for i, (dx, dy) in enumerate(XY):
        wg.append(
            send(fw.at[mine], fw.at[mine], s_wg.at[i], r_wg.at[me_p], plane_dev(plane(dx, dy)))
        )

    for dx, dy in XY:
        p = plane(dx, dy)
        part = pl.ds(pl.multiple_of(p * PR_ROWS, PR_ROWS), PR_ROWS)
        arrival(fg.at[c, part], s_qg.at[0], r_qg.at[p]).wait_recv()
    qc = send(fg.at[c], fg.at[c], s_qc, r_qc, sibling)
    qc.wait_recv()
    for dx, dy in XY:
        p = plane(dx, dy)
        arrival(fw.at[pl.ds(pl.multiple_of(c * GH + p * GR, GR), GR)], s_wg.at[0], r_wg.at[p]).wait_recv()
    half = pl.ds(pl.multiple_of(c * GH, GH), GH)
    wc = send(fw.at[half], fw.at[half], s_wc, r_wc, sibling)
    wc.wait_recv()
    out_f = pltpu.make_async_copy(fg, gproto_out, s_in.at[0])
    out_w = pltpu.make_async_copy(fw, gweight_out, s_in.at[1])
    out_f.start()
    out_w.start()
    out_f.wait()
    out_w.wait()

    for copy in pending:
        copy.wait_send()


def finish(batch_rows, fg, fw, protos, gproto_out, gweight_out, loss_out):
    g = jnp.concatenate([fg[0], fg[1]], axis=1)[0:KS, :]
    own = protos[...]
    pinv = lax.rsqrt(jnp.sum(own * own, axis=-1, keepdims=True) + TINY)
    u = own * pinv
    along = jnp.sum(u * g, axis=-1, keepdims=True)
    gproto_out[...] = (g - u * along) * pinv
    gweight_out[...] = fw[...]
    loss_out[...] = fg[0, KP - 1 : KP, 0:1] * (-1.0 / (2.0 * batch_rows))


def body(features, projection, prototypes):
    rows = features.shape[0]
    batch_rows = rows * lax.axis_size("dp")
    dma = pltpu.SemaphoreType.DMA
    nxy, nz = len(XY), len(ZO)
    vm = pltpu.VMEM
    scratch = [
        vm((WR, 2, E), BF), vm((2, WR, E), BF), vm((E, D), BF), vm((KS, D), F32), dma((3,)),
        vm((KP, D), F32), vm((NZ, NQ, NC, QR, D), BF), vm((2 * WR, D), F32), vm((2 * WR, 1), F32),
        vm((3 * WR, D), BF), vm((NZ, 2 * WR, D), BF), vm((E, 2 * WR), BF),
        vm((NZ, 3 * WR, KP), F32), vm((NZ, 2 * WR, KP), F32), vm((NZ, 2 * WR, KP), F32), vm((NZ, KP, 2 * WR), F32),
        vm((2 * WR, 1), F32), vm((2 * WR, 1), F32), vm((NZ, 8, KP), F32), vm((3, NT, 128), F32), vm((3, NT, 128), F32),
        vm((NT, 128), F32), vm((NZ, 2 * WR, KP), BF),
        vm((3, nxy, NT, 128), F32), vm((3, nz, NT, 128), F32), vm((3, NT, 128), F32),
        vm((2 * WR, D), F32), vm((NZ, KP, 2 * WR), BF), vm((2, KP, 128), F32), vm((NZ, 8, 128), F32), vm((NZ, 8, 128), F32),
        vm((KP, D), F32), vm((KP, DH), F32), vm((KP, DH), F32), vm((nxy, PR_ROWS, DH), F32), vm((NC, KP, DH), F32),
        vm((E, D), F32), vm((GH, D), F32), vm((GH, D), F32), vm((nxy, GR, D), F32), vm((NZ, GR, D), F32), vm((E, D), F32),
        vm((8, 128), F32),
        dma((nz,)), dma((nz,)), dma((len(FAR), len(NB))), dma((len(FAR), len(NB))), dma((nz,)), dma((nz,)), dma, dma,
        dma((3, nxy)), dma((3, nxy)), dma((3, nz)), dma((3, nz)), dma, dma,
        dma((4, 2)), dma((4, 2)), dma((nz,)), dma((NZ,)), dma((nz,)), dma((NZ,)), dma, dma,
        dma((nxy,)), dma((nxy,)), dma((nxy,)), dma((NP,)), dma, dma,
        dma, dma, dma((nxy,)), dma((nxy,)), dma((nz,)), dma((NZ,)), dma((nxy,)), dma((NP,)), dma, dma,
    ]
    vspec = pl.BlockSpec(memory_space=pltpu.VMEM)
    aspec = pl.BlockSpec(memory_space=pl.ANY)
    fg, fw = pl.pallas_call(
        functools.partial(kernel, batch_rows),
        out_shape=(
            jax.ShapeDtypeStruct((NC, KP, DH), F32),
            jax.ShapeDtypeStruct((E, D), F32),
        ),
        in_specs=[aspec] * 3,
        out_specs=(aspec,) * 2,
        scratch_shapes=scratch,
        compiler_params=pltpu.CompilerParams(
            collective_id=0, has_side_effects=True, vmem_limit_bytes=VLIM * 1024 * 1024
        ),
        name="swav",
    )(features, projection, prototypes)
    gproto, gweight, loss = pl.pallas_call(
        functools.partial(finish, batch_rows),
        out_shape=(
            jax.ShapeDtypeStruct((KS, D), F32),
            jax.ShapeDtypeStruct((E, D), F32),
            jax.ShapeDtypeStruct((1, 1), F32),
        ),
        in_specs=[vspec] * 3,
        out_specs=(vspec,) * 3,
        name="finish",
    )(fg, fw, prototypes)
    return gproto, gweight, loss.reshape(())


def solution(mesh):
    return jax.shard_map(
        body,
        mesh=mesh,
        in_specs=(P("dp", None, None), P(), P("mp", None)),
        out_specs=(P("mp", None), P(), P()),
        check_vma=False,
    )
```

```python
import functools

import jax
import jax.numpy as jnp
from jax import lax
from jax.experimental import pallas as pl
from jax.experimental.pallas import tpu as pltpu
from jax.sharding import PartitionSpec as P

MESH = pl.DeviceIdType.MESH
BF = jnp.bfloat16
F32 = jnp.float32

EPSILON_CODES = 0.05
SOFTMAX_TEMPER = 0.1
LOSS_FACTOR = 4096.0
VLIM = 60
TINY = 1e-06

NX, NY, NC, NZ = 4, 4, 2, 8
NP = NX * NY
KS = 375
KP = 384
LT = KP // 128
NT = NZ * LT
WR = 256
D = 256
E = 512
NQ = 4
QR = KP // NQ // NC
DH = D // 2
PR_ROWS = KP // NP
GH = E // 2
NH = 1
GQ = GH // NH
GR = GQ // NP
XY = [(dx, dy) for dx in range(NX) for dy in range(NY) if dx or dy]
ZO = [1, 7, 2, 6, 3, 5, 4]
FAR = [4, 3, 5, 2, 6]
NEAR = [1, 7]
NB = [(1, 0), (-1, 0), (0, 1)]


def nt_dot(a, b):
    return lax.dot_general(a, b, (((1,), (1,)), ((), ())), preferred_element_type=F32)


def dot(a, b):
    return jnp.dot(a, b, preferred_element_type=F32)


def kernel(
    batch_rows,
    feats_in, weight_in, protos_in,
    gproto_out, gweight_out,
    raw, feats, weight, protos, s_in,
    pu, ph, unit, inv, emb, emb_line, xt,
    ex, sc, so, so_line, den, rsc, acc, vec, csum, cothers, gm,
    buf_a, buf_b, vec_b,
    eg, gm_line, col, lanes, share_z, pg, buf_p, pr, buf_q, fg, gw, buf_w, buf_x, buf_y, fw, loss_acc,
    s_x1, s_x2, s_z1, s_z2, s_f, s_m,
    r_z, r_n, r_f, r_e, r_a, r_b, r_c, r_l, r_v, r_h, r_p, r_q, r_qg, r_qc, r_w, r_wx, r_wz, r_wg, r_wc,
):
    dp = lax.axis_index("dp")
    z = lax.axis_index("mp")
    x, y, c = dp // (NY * NC), (dp // NC) % NY, dp % NC
    o = 1 - c
    me_p = x * NY + y
    gf = LOSS_FACTOR / (2.0 * batch_rows * SOFTMAX_TEMPER)
    pools = {"x1": s_x1, "x2": s_x2, "z1": s_z1, "z2": s_z2, "f": s_f, "m": s_m}
    pending = {}

    def plane(dx, dy):
        px, py = (x + dx) % NX, (y + dy) % NY
        return px * NY + py

    def plane_dev(p):
        return {"dp": p * NC + c, "mp": z}

    def z_dev(dz):
        return {"dp": dp, "mp": (z + dz) % NZ}

    sibling = {"dp": dp + 1 - 2 * c, "mp": z}

    def send(src, dst, key, rsem, device):
        if key in pending:
            pending.pop(key).wait_send()
        copy = pltpu.make_async_remote_copy(
            src_ref=src, dst_ref=dst, send_sem=pools[key[0]].at[key[1]], recv_sem=rsem,
            device_id=device, device_id_type=MESH,
        )
        copy.start()
        pending[key] = copy
        return copy

    def arrival(dst, rsem):
        return pltpu.make_async_remote_copy(
            src_ref=dst, dst_ref=dst, send_sem=s_m.at[0], recv_sem=rsem, device_id=sibling, device_id_type=MESH
        )

    barrier = pltpu.get_barrier_semaphore()
    pl.semaphore_signal(barrier, inc=1, device_id=sibling, device_id_type=MESH)
    for dx, dy in XY:
        pl.semaphore_signal(barrier, inc=1, device_id=plane_dev(plane(dx, dy)), device_id_type=MESH)
    for dz in ZO:
        pl.semaphore_signal(barrier, inc=1, device_id=z_dev(dz), device_id_type=MESH)

    loads = [
        pltpu.make_async_copy(protos_in, protos, s_in.at[0]),
        pltpu.make_async_copy(feats_in.at[pl.ds(z * WR, WR)], raw, s_in.at[1]),
        pltpu.make_async_copy(weight_in, weight, s_in.at[2]),
    ]
    for load in loads:
        load.start()

    loads[0].wait()
    pu[...] = jnp.zeros_like(pu)
    own = protos[...]
    pu[0:KS, :] = own * lax.rsqrt(jnp.sum(own * own, axis=-1, keepdims=True) + TINY)
    ph[z] = pu[...].astype(BF).reshape(NQ, NC, QR, D)
    pl.semaphore_wait(barrier, 1 + len(XY) + len(ZO))

    colour = (x + 2 * y) % NQ
    for i, dz in enumerate(FAR):
        part = ph.at[z, colour, c]
        send(part, part, ("z1", i), r_z.at[i], z_dev(dz))
    for i, dz in enumerate(NEAR):
        part = ph.at[z, :, c]
        send(part, part, ("z1", len(FAR) + i), r_z.at[len(FAR) + i], z_dev(dz))

    def slab(q):
        return ph[q].reshape(KP, D)

    loads[1].wait()
    loads[2].wait()
    to = lax.broadcasted_iota(jnp.int32, (2 * WR, 2 * WR), 0)
    fro = lax.broadcasted_iota(jnp.int32, (2 * WR, 2 * WR), 1)
    order = ((to % WR) * 2 + to // WR == fro).astype(F32).astype(BF)
    feats[...] = dot(order, raw[...].reshape(2 * WR, E)).astype(BF).reshape(2, WR, E)

    def embed(view, row, erow):
        raw = dot(feats[view], weight[...])
        inverse = lax.rsqrt(jnp.sum(raw * raw, axis=-1, keepdims=True) + TINY)
        u = raw * inverse
        inv[row : row + WR, :] = inverse
        unit[row : row + WR, :] = u
        emb[erow : erow + WR, :] = u.astype(BF)

    embed(o, WR, 2 * WR)
    ecopy = send(emb.at[pl.ds(2 * WR, WR)], emb.at[pl.ds(WR, WR)], ("m", 0), r_e, sibling)
    embed(c, 0, 0)
    ecopy.wait_recv()

    def scores_slab(q):
        pq_ = slab(q)
        tot = jnp.zeros((8, KP), F32)
        for b in range(2):
            s = nt_dot(emb[b * WR : (b + 1) * WR, :], pq_)
            e = jnp.exp(s * (1.0 / EPSILON_CODES))
            ex[q, b * WR : (b + 1) * WR, :] = e
            if b == 0:
                sc[q, 0:WR, :] = s
            tot = tot + jnp.sum(e.reshape(WR // 8, 8, KP), axis=0)
        acc[q] = tot

    scores_slab(z)
    came = [(z + NZ - dz) % NZ for dz in FAR + NEAR]
    for i in range(len(FAR)):
        part = ph.at[came[i], colour, c]
        arrival(part, r_z.at[i]).wait_recv()
        for n, (dx, dy) in enumerate(NB):
            send(part, part, ("x2", i * len(NB) + n), r_n.at[i, n], plane_dev(plane(dx, dy)))

    def to_sibling(i):
        part = ph.at[came[i], :, c]
        return send(part, part, ("f", i), r_f.at[i], sibling)

    forwards = {}
    for i in (len(FAR), len(FAR) + 1):
        arrival(ph.at[came[i], :, c], r_z.at[i]).wait_recv()
        forwards[i] = to_sibling(i)
    for i in (len(FAR), len(FAR) + 1):
        forwards[i].wait_recv()
        scores_slab(came[i])
    for i in range(len(FAR) + 1):
        if i < len(FAR):
            for n, (dx, dy) in enumerate(NB):
                part = ph.at[came[i], (colour + 3 * NQ - dx - 2 * dy) % NQ, c]
                arrival(part, r_n.at[i, n]).wait_recv()
            forwards[i] = to_sibling(i)
        if i:
            forwards[i - 1].wait_recv()
            scores_slab(came[i - 1])

    lane = lax.broadcasted_iota(jnp.int32, (NT, 128), 1)
    row = lax.broadcasted_iota(jnp.int32, (NT, 128), 0)
    valid = lane + (row % LT) * 128 < KS

    def finish_column_sums(k):
        for q in range(NZ):
            part = jnp.sum(acc[q], axis=0, keepdims=True)
            for j in range(LT):
                vec[k, q * LT + j : q * LT + j + 1, :] = part[:, j * 128 : (j + 1) * 128]

    def reduce_columns(k, work_a, work_b):
        finish_column_sums(k)
        copies = []
        for i, (dx, dy) in enumerate(XY):
            copies.append(
                send(vec.at[k], buf_a.at[k, i], ("x1", i), r_a.at[k], plane_dev(plane(dx, dy)))
            )
        work_a()
        total = vec[k]
        arrival(buf_a.at[k], r_a.at[k]).wait_recv()
        for i in range(len(XY)):
            total = total + buf_a[k, i]
        vec_b[k] = total
        copies = []
        for i, dz in enumerate(ZO):
            copies.append(send(vec_b.at[k], buf_b.at[k, i], ("z1", i), r_b.at[k], z_dev(dz)))
        work_b()
        arrival(buf_b.at[k], r_b.at[k]).wait_recv()
        for i in range(len(ZO)):
            total = total + buf_b[k, i]
        csum[k] = jnp.where(valid, 1.0 / total, 0.0)

    def other_view():
        def step(q, carry):
            s = nt_dot(emb[2 * WR : 3 * WR, :], slab(q))
            ex[q, 2 * WR : 3 * WR, :] = jnp.exp(s * (1.0 / EPSILON_CODES))
            sc[q, WR : 2 * WR, :] = s
            return carry

        lax.fori_loop(0, NZ, step, 0)

    last = lax.broadcasted_iota(jnp.int32, (1, 128), 1) < KS - (LT - 1) * 128

    def denominators(first):
        R = 64

        def step(b, carry):
            rows = pl.ds(pl.multiple_of(first + b * R, R), R)
            total = jnp.zeros((R, 128), F32)
            for q in range(NZ):
                s = jnp.exp(sc[q, rows, :] * (1.0 / SOFTMAX_TEMPER))
                so[q, rows, :] = s
                for j in range(LT):
                    part = s[:, j * 128 : (j + 1) * 128]
                    if j == LT - 1:
                        part = jnp.where(last, part, 0.0)
                    total = total + part
            den[rows, :] = jnp.sum(total, axis=1, keepdims=True)
            return carry

        lax.fori_loop(0, WR // R, step, 0)

    def line_slot(dz):
        return (z + NZ + dz) % NZ

    def line_step(n):
        for i, way in enumerate((1, -1)):
            slot = line_slot(-way * (n - 1))
            part = emb_line.at[slot]
            if n == NZ // 2:
                part = emb_line.at[slot, pl.ds(i * WR, WR)]
            send(part, part, ("m", 2 + i), r_l.at[n - 1, i], z_dev(way % NZ))

    def line_wait(n):
        for i, way in enumerate((1, -1)):
            slot = line_slot(-way * n)
            part = emb_line.at[slot]
            if n == NZ // 2:
                part = emb_line.at[slot, pl.ds(i * WR, WR)]
            arrival(part, r_l.at[n - 1, i]).wait_recv()

    def line_scores(dz):
        slot = line_slot(dz)
        s = nt_dot(slab(z), emb_line[slot])
        so_line[slot] = jnp.exp(s * (1.0 / SOFTMAX_TEMPER))

    eye = lax.broadcasted_iota(jnp.int32, (128, 128), 0) == lax.broadcasted_iota(jnp.int32, (128, 128), 1)

    def to_lanes(ref, row):
        for i in range(2 * WR // 128):
            part = jnp.broadcast_to(ref[i * 128 : (i + 1) * 128, :], (128, 128))
            lanes[z, row + i : row + i + 1, :] = jnp.sum(jnp.where(eye, part, 0.0), axis=0, keepdims=True)

    def row_inverse(cs, rows, R):
        total = jnp.zeros((R, 128), F32)
        for q in range(NZ):
            for j in range(LT):
                t = q * LT + j
                total = total + ex[q, rows, j * 128 : (j + 1) * 128] * cs[t : t + 1, :]
        return 1.0 / jnp.sum(total, axis=1, keepdims=True)

    def sinkhorn_pass(k):
        R = 128
        acc[...] = jnp.zeros_like(acc)

        def step(b, carry):
            rows = pl.ds(pl.multiple_of(b * R, R), R)
            r = row_inverse(csum.at[k], rows, R)
            for q in range(NZ):
                t = ex[q, rows, :] * r
                acc[q] += jnp.sum(t.reshape(R // 8, 8, KP), axis=0)
            return carry

        lax.fori_loop(0, 2 * WR // R, step, 0)

    def nothing():
        pass

    emb_line[z, 0:WR, :] = emb[0:WR, :]
    emb_line[z, WR : 2 * WR, :] = emb[2 * WR : 3 * WR, :]

    def work_1a():
        line_step(1)
        other_view()
        line_scores(0)

    def work_2b():
        line_scores(-1)
        line_scores(1)
        to_lanes(den, 4)

    def work_3a():
        line_scores(-2)

    def work_1b():
        denominators(0)
        xt[:, 0:WR] = feats[c].astype(F32).T.astype(BF)

    def work_2a():
        denominators(WR)
        xt[:, WR : 2 * WR] = feats[o].astype(F32).T.astype(BF)

    reduce_columns(0, work_1a, work_1b)
    line_wait(1)
    line_step(2)
    sinkhorn_pass(0)
    reduce_columns(1, work_2a, work_2b)
    line_wait(2)
    line_step(3)
    sinkhorn_pass(1)
    reduce_columns(2, work_3a, lambda: line_scores(2))
    ccopy = send(csum.at[2], cothers, ("m", 1), r_c, sibling)
    line_wait(3)
    line_step(4)

    def row_scales(cs, row, erow):
        def step(b, carry):
            R = 64
            rows = pl.ds(pl.multiple_of(row + b * R, R), R)
            rsc[rows, :] = row_inverse(cs, pl.ds(pl.multiple_of(erow + b * R, R), R), R)
            return carry

        lax.fori_loop(0, WR // 64, step, 0)

    row_scales(csum.at[2], 0, 0)
    ccopy.wait_recv()
    row_scales(cothers, WR, 2 * WR)
    to_lanes(rsc, 0)
    for i, dz in enumerate(ZO):
        send(lanes.at[z], lanes.at[z], ("z1", i), r_v.at[z], z_dev(dz))

    RG = 32
    loss_acc[...] = jnp.zeros_like(loss_acc)

    def grad_step(b, carry):
        rows_c = pl.ds(pl.multiple_of(b * RG, RG), RG)
        rows_o = pl.ds(pl.multiple_of(WR + b * RG, RG), RG)
        erows_o = pl.ds(pl.multiple_of(2 * WR + b * RG, RG), RG)
        rc = rsc[rows_c, :] * gf
        ro = rsc[rows_o, :] * gf
        dc = gf / den[rows_c, :]
        do = gf / den[rows_o, :]
        total = jnp.zeros((RG, 128), F32)
        for q in range(NZ):
            for j in range(LT):
                t = q * LT + j
                cols = slice(j * 128, (j + 1) * 128)
                ac = ex[q, rows_c, cols] * csum[2, t : t + 1, :] * rc
                ao = ex[q, erows_o, cols] * cothers[t : t + 1, :] * ro
                gm[rows_c, t * 128 : (t + 1) * 128] = (so[q, rows_c, cols] * dc - ao).astype(BF)
                gm[rows_o, t * 128 : (t + 1) * 128] = (so[q, rows_o, cols] * do - ac).astype(BF)
                total = total + ao * sc[q, rows_c, cols] + ac * sc[q, rows_o, cols]
        loss_acc[...] += jnp.sum(total.reshape(RG // 8, 8, 128), axis=0)
        return carry

    lax.fori_loop(0, WR // RG, grad_step, 0)

    log_total = jnp.sum(jnp.log(den[...]))
    share = jnp.sum(loss_acc[...]) * (1.0 / (SOFTMAX_TEMPER * gf)) - log_total
    share_z[z] = jnp.full((8, 128), share, F32)
    for i, dz in enumerate(ZO):
        send(share_z.at[z], share_z.at[z], ("z2", i), r_h.at[z], z_dev(dz))

    eg[...] = dot(gm[...], ph[...].reshape(NZ * KP, D))
    along = jnp.sum(unit[...] * eg[...], axis=-1, keepdims=True)
    graw = ((eg[...] - unit[...] * along) * inv[...]).astype(BF)
    def half_rows(h, core):
        return pl.ds(pl.multiple_of((h * NC + core) * GQ, GQ), GQ)

    def own_rows(h, p):
        return pl.ds(pl.multiple_of((h * NC + c) * GQ + p * GR, GR), GR)

    wcopy = []
    for h in range(NH):
        theirs = half_rows(h, o)
        gw[theirs, :] = dot(xt[theirs, :], graw)
        wcopy.append(send(gw.at[theirs], buf_w.at[h], ("m", 6 + 2 * h), r_w.at[h], sibling))
    wcopies = []
    for h in range(NH):
        ours = half_rows(h, c)
        grads = dot(xt[ours, :], graw)
        wcopy[h].wait_recv()
        gw[ours, :] = grads + buf_w[h]
        for i, (dx, dy) in enumerate(XY):
            p = plane(dx, dy)
            wcopies.append(
                send(gw.at[own_rows(h, p)], buf_x.at[h, i], ("x1", i), r_wx.at[h], plane_dev(p))
            )

    for v, cs in enumerate((csum.at[2], cothers)):
        for j in range(LT):
            part = jnp.broadcast_to(cs[pl.ds(z * LT + j, 1), :], (128, 128))
            part = jnp.sum(jnp.where(eye, part, 0.0), axis=1, keepdims=True)
            col[v, j * 128 : (j + 1) * 128, :] = jnp.broadcast_to(part, (128, 128))
    line_scores(-3)
    line_scores(3)
    line_wait(4)
    line_scores(4)
    for dz in ZO:
        k = line_slot(dz)
        arrival(lanes.at[k], r_v.at[k]).wait_recv()

    def line_grad(k, carry):
        scale = [lanes[k, i : i + 1, :] * gf for i in range(4)]
        soft = [gf / lanes[k, i : i + 1, :] for i in range(4, 8)]
        R = 32
        for b in range(KP // R):
            rows = slice(b * R, (b + 1) * R)
            for i in range(2):
                lc, lo = slice(i * 128, (i + 1) * 128), slice(WR + i * 128, WR + (i + 1) * 128)
                sc_, so_ = so_line[k, rows, lc], so_line[k, rows, lo]
                ac = sc_ * sc_ * col[0, rows, :] * scale[i]
                ao = so_ * so_ * col[1, rows, :] * scale[2 + i]
                gm_line[k, rows, lc] = (sc_ * soft[i] - ao).astype(BF)
                gm_line[k, rows, lo] = (so_ * soft[2 + i] - ac).astype(BF)
        return carry

    lax.fori_loop(0, NZ, line_grad, 0)
    grads = jnp.zeros((KP, D), F32)
    for k in range(NZ):
        grads = grads + dot(gm_line[k], emb_line[k])
    pg[...] = grads
    for dz in ZO:
        k = line_slot(dz)
        arrival(share_z.at[k], r_h.at[k]).wait_recv()
    share = share_z[0, 0:1, 0:1]
    for k in range(1, NZ):
        share = share + share_z[k, 0:1, 0:1]
    spare = lax.broadcasted_iota(jnp.int32, (8, D), 0) == 7
    pg[KP - 8 : KP, :] = jnp.where(spare, share, pg[KP - 8 : KP, :])
    pcopy = send(pg.at[:, pl.ds(pl.multiple_of(o * DH, DH), DH)], buf_p, ("m", 4), r_p, sibling)
    pcopy.wait_recv()
    pr[...] = pg[:, pl.ds(pl.multiple_of(c * DH, DH), DH)] + buf_p[...]
    qcopies = []
    for i, (dx, dy) in enumerate(XY):
        p = plane(dx, dy)
        qcopies.append(
            send(pr.at[pl.ds(pl.multiple_of(p * PR_ROWS, PR_ROWS), PR_ROWS)], buf_q.at[i], ("x2", i), r_q, plane_dev(p))
        )

    for h in range(NH):
        total = gw[own_rows(h, me_p), :]
        arrival(buf_x.at[h], r_wx.at[h]).wait_recv()
        for i in range(len(XY)):
            total = total + buf_x[h, i]
        buf_y[h, z] = total
        for i, dz in enumerate(ZO):
            send(buf_y.at[h, z], buf_y.at[h, z], ("z1", i), r_wz.at[h, z], z_dev(dz))

    mine_p = pl.ds(pl.multiple_of(me_p * PR_ROWS, PR_ROWS), PR_ROWS)
    total = pr[mine_p, :]
    arrival(buf_q, r_q).wait_recv()
    for i in range(len(XY)):
        total = total + buf_q[i]
    fg[c, mine_p, :] = total
    for i, (dx, dy) in enumerate(XY):
        send(fg.at[c, mine_p], fg.at[c, mine_p], ("x2", i), r_qg.at[me_p], plane_dev(plane(dx, dy)))

    for h in range(NH):
        for dz in ZO:
            k = line_slot(dz)
            arrival(buf_y.at[h, k], r_wz.at[h, k]).wait_recv()
        total = buf_y[h, 0]
        for k in range(1, NZ):
            total = total + buf_y[h, k]
        part = own_rows(h, me_p)
        fw[part, :] = total
        for i, (dx, dy) in enumerate(XY):
            send(fw.at[part], fw.at[part], ("x1", i), r_wg.at[h, me_p], plane_dev(plane(dx, dy)))

    for dx, dy in XY:
        p = plane(dx, dy)
        part = fg.at[c, pl.ds(pl.multiple_of(p * PR_ROWS, PR_ROWS), PR_ROWS)]
        arrival(part, r_qg.at[p]).wait_recv()
    send(fg.at[c], fg.at[c], ("m", 5), r_qc, sibling).wait_recv()
    out_f = pltpu.make_async_copy(fg, gproto_out, s_in.at[0])
    out_f.start()

    forwards = []
    for h in range(NH):
        for i, (dx, dy) in enumerate(XY):
            p = plane(dx, dy)
            arrival(fw.at[own_rows(h, p)], r_wg.at[h, p]).wait_recv()
        part = fw.at[half_rows(h, c)]
        forwards.append(send(part, part, ("m", 7 + 2 * h), r_wc.at[h], sibling))
    for copy in forwards:
        copy.wait_recv()
    out_w = pltpu.make_async_copy(fw, gweight_out, s_in.at[1])
    out_w.start()
    out_f.wait()
    out_w.wait()

    for copy in pending.values():
        copy.wait_send()


def finish(batch_rows, fg, fw, protos, gproto_out, gweight_out, loss_out):
    g = jnp.concatenate([fg[0], fg[1]], axis=1)[0:KS, :]
    own = protos[...]
    pinv = lax.rsqrt(jnp.sum(own * own, axis=-1, keepdims=True) + TINY)
    u = own * pinv
    along = jnp.sum(u * g, axis=-1, keepdims=True)
    gproto_out[...] = (g - u * along) * pinv
    gweight_out[...] = fw[...]
    loss_out[...] = fg[0, KP - 1 : KP, 0:1] * (-1.0 / (2.0 * batch_rows))


def body(features, projection, prototypes):
    rows = features.shape[0]
    batch_rows = rows * lax.axis_size("dp")
    dma = pltpu.SemaphoreType.DMA
    nxy, nz = len(XY), len(ZO)
    vm = pltpu.VMEM
    scratch = [
        vm((WR, 2, E), BF), vm((2, WR, E), BF), vm((E, D), BF), vm((KS, D), F32), dma((3,)),
        vm((KP, D), F32), vm((NZ, NQ, NC, QR, D), BF), vm((2 * WR, D), F32), vm((2 * WR, 1), F32),
        vm((3 * WR, D), BF), vm((NZ, 2 * WR, D), BF), vm((E, 2 * WR), BF),
        vm((NZ, 3 * WR, KP), F32), vm((NZ, 2 * WR, KP), F32), vm((NZ, 2 * WR, KP), F32), vm((NZ, KP, 2 * WR), F32),
        vm((2 * WR, 1), F32), vm((2 * WR, 1), F32), vm((NZ, 8, KP), F32), vm((3, NT, 128), F32), vm((3, NT, 128), F32),
        vm((NT, 128), F32), vm((2 * WR, NZ * KP), BF),
        vm((3, nxy, NT, 128), F32), vm((3, nz, NT, 128), F32), vm((3, NT, 128), F32),
        vm((2 * WR, D), F32), vm((NZ, KP, 2 * WR), BF), vm((2, KP, 128), F32), vm((NZ, 8, 128), F32), vm((NZ, 8, 128), F32),
        vm((KP, D), F32), vm((KP, DH), F32), vm((KP, DH), F32), vm((nxy, PR_ROWS, DH), F32), vm((NC, KP, DH), F32),
        vm((E, D), F32), vm((NH, GQ, D), F32), vm((NH, nxy, GR, D), F32), vm((NH, NZ, GR, D), F32), vm((E, D), F32),
        vm((8, 128), F32),
        dma((nxy,)), dma((nxy,)), dma((nz,)), dma((nz,)), dma((nz,)), dma((6 + 2 * NH,)),
        dma((nz,)), dma((len(FAR), len(NB))), dma((nz,)), dma, dma((3,)), dma((3,)), dma, dma((4, 2)), dma((NZ,)),
        dma((NZ,)), dma, dma, dma((NP,)), dma, dma((NH,)), dma((NH,)), dma((NH, NZ)), dma((NH, NP)), dma((NH,)),
    ]
    vspec = pl.BlockSpec(memory_space=pltpu.VMEM)
    aspec = pl.BlockSpec(memory_space=pl.ANY)
    fg, fw = pl.pallas_call(
        functools.partial(kernel, batch_rows),
        out_shape=(
            jax.ShapeDtypeStruct((NC, KP, DH), F32),
            jax.ShapeDtypeStruct((E, D), F32),
        ),
        in_specs=[aspec] * 3,
        out_specs=(aspec,) * 2,
        scratch_shapes=scratch,
        compiler_params=pltpu.CompilerParams(
            collective_id=0, has_side_effects=True, vmem_limit_bytes=VLIM * 1024 * 1024
        ),
        name="swav",
    )(features, projection, prototypes)
    gproto, gweight, loss = pl.pallas_call(
        functools.partial(finish, batch_rows),
        out_shape=(
            jax.ShapeDtypeStruct((KS, D), F32),
            jax.ShapeDtypeStruct((E, D), F32),
            jax.ShapeDtypeStruct((1, 1), F32),
        ),
        in_specs=[vspec] * 3,
        out_specs=(vspec,) * 3,
        name="finish",
    )(fg, fw, prototypes)
    return gproto, gweight, loss.reshape(())


def solution(mesh):
    return jax.shard_map(
        body,
        mesh=mesh,
        in_specs=(P("dp", None, None), P(), P("mp", None)),
        out_specs=(P("mp", None), P(), P()),
        check_vma=False,
    )
```

```python
import functools

import jax
import jax.numpy as jnp
from jax import lax
from jax.experimental import pallas as pl
from jax.experimental.pallas import tpu as pltpu
from jax.sharding import PartitionSpec as P

MESH = pl.DeviceIdType.MESH
BF = jnp.bfloat16
F32 = jnp.float32

EPSILON_CODES = 0.05
SOFTMAX_TEMPER = 0.1
LOSS_FACTOR = 4096.0
VLIM = 60
TINY = 1e-06

NX, NY, NC, NZ = 4, 4, 2, 8
NP = NX * NY
KS = 375
KP = 384
LT = KP // 128
NT = NZ * LT
WR = 256
D = 256
E = 512
NQ = 4
QR = KP // NQ // NC
DH = D // 2
PR_ROWS = KP // NP
GH = E // 2
NH = 1
GQ = GH // NH
GR = GQ // NP
XY = [(dx, dy) for dx in range(NX) for dy in range(NY) if dx or dy]
ZO = [1, 7, 2, 6, 3, 5, 4]
FAR = [4, 3, 5, 2, 6]
NEAR = [1, 7]
NB = [(1, 0), (-1, 0), (0, 1)]


def nt_dot(a, b):
    return lax.dot_general(a, b, (((1,), (1,)), ((), ())), preferred_element_type=F32)


def dot(a, b):
    return jnp.dot(a, b, preferred_element_type=F32)


def kernel(
    batch_rows,
    feats_in, weight_in, protos_in,
    gproto_out, gweight_out,
    raw, feats, weight, protos, s_in,
    pu, ph, unit, inv, emb, emb_line, xt,
    ex, sc, so, so_line, den, rsc, acc, vec, csum, cothers, gm,
    buf_a, buf_b, vec_b,
    eg, gm_line, col, lanes, share_z, pg, buf_p, pr, buf_q, fg, gw, buf_w, buf_x, buf_y, fw, loss_acc,
    s_x1, s_x2, s_z1, s_z2, s_f, s_m,
    r_z, r_n, r_f, r_e, r_a, r_b, r_c, r_l, r_v, r_h, r_p, r_q, r_qg, r_qc, r_w, r_wx, r_wz, r_wg, r_wc,
):
    dp = lax.axis_index("dp")
    z = lax.axis_index("mp")
    x, y, c = dp // (NY * NC), (dp // NC) % NY, dp % NC
    o = 1 - c
    me_p = x * NY + y
    gf = LOSS_FACTOR / (2.0 * batch_rows * SOFTMAX_TEMPER)
    pools = {"x1": s_x1, "x2": s_x2, "z1": s_z1, "z2": s_z2, "f": s_f, "m": s_m}
    pending = {}

    def plane(dx, dy):
        px, py = (x + dx) % NX, (y + dy) % NY
        return px * NY + py

    def plane_dev(p):
        return {"dp": p * NC + c, "mp": z}

    def z_dev(dz):
        return {"dp": dp, "mp": (z + dz) % NZ}

    sibling = {"dp": dp + 1 - 2 * c, "mp": z}

    def send(src, dst, key, rsem, device):
        if key in pending:
            pending.pop(key).wait_send()
        copy = pltpu.make_async_remote_copy(
            src_ref=src, dst_ref=dst, send_sem=pools[key[0]].at[key[1]], recv_sem=rsem,
            device_id=device, device_id_type=MESH,
        )
        copy.start()
        pending[key] = copy
        return copy

    def arrival(dst, rsem):
        return pltpu.make_async_remote_copy(
            src_ref=dst, dst_ref=dst, send_sem=s_m.at[0], recv_sem=rsem, device_id=sibling, device_id_type=MESH
        )

    barrier = pltpu.get_barrier_semaphore()
    pl.semaphore_signal(barrier, inc=1, device_id=sibling, device_id_type=MESH)
    for dx, dy in XY:
        pl.semaphore_signal(barrier, inc=1, device_id=plane_dev(plane(dx, dy)), device_id_type=MESH)
    for dz in ZO:
        pl.semaphore_signal(barrier, inc=1, device_id=z_dev(dz), device_id_type=MESH)

    loads = [
        pltpu.make_async_copy(protos_in, protos, s_in.at[0]),
        pltpu.make_async_copy(feats_in.at[pl.ds(z * WR, WR)], raw, s_in.at[1]),
        pltpu.make_async_copy(weight_in, weight, s_in.at[2]),
    ]
    for load in loads:
        load.start()

    loads[0].wait()
    pu[...] = jnp.zeros_like(pu)
    own = protos[...]
    pu[0:KS, :] = own * lax.rsqrt(jnp.sum(own * own, axis=-1, keepdims=True) + TINY)
    ph[z] = pu[...].astype(BF).reshape(NQ, NC, QR, D)
    pl.semaphore_wait(barrier, 1 + len(XY) + len(ZO))

    colour = (x + 2 * y) % NQ
    for i, dz in enumerate(FAR):
        part = ph.at[z, colour, c]
        send(part, part, ("z1", i), r_z.at[i], z_dev(dz))
    for i, dz in enumerate(NEAR):
        part = ph.at[z, :, c]
        send(part, part, ("z1", len(FAR) + i), r_z.at[len(FAR) + i], z_dev(dz))

    def slab(q):
        return ph[q].reshape(KP, D)

    loads[1].wait()
    loads[2].wait()
    to = lax.broadcasted_iota(jnp.int32, (2 * WR, 2 * WR), 0)
    fro = lax.broadcasted_iota(jnp.int32, (2 * WR, 2 * WR), 1)
    order = ((to % WR) * 2 + to // WR == fro).astype(F32).astype(BF)
    feats[...] = dot(order, raw[...].reshape(2 * WR, E)).astype(BF).reshape(2, WR, E)

    def embed(view, row, erow):
        raw = dot(feats[view], weight[...])
        inverse = lax.rsqrt(jnp.sum(raw * raw, axis=-1, keepdims=True) + TINY)
        u = raw * inverse
        inv[row : row + WR, :] = inverse
        unit[row : row + WR, :] = u
        emb[erow : erow + WR, :] = u.astype(BF)

    embed(o, WR, 2 * WR)
    ecopy = send(emb.at[pl.ds(2 * WR, WR)], emb.at[pl.ds(WR, WR)], ("m", 0), r_e, sibling)
    embed(c, 0, 0)
    ecopy.wait_recv()

    def scores_slab(q):
        pq_ = slab(q)
        tot = jnp.zeros((8, KP), F32)
        for b in range(2):
            s = nt_dot(emb[b * WR : (b + 1) * WR, :], pq_)
            e = jnp.exp(s * (1.0 / EPSILON_CODES))
            ex[q, b * WR : (b + 1) * WR, :] = e
            if b == 0:
                sc[q, 0:WR, :] = s
            tot = tot + jnp.sum(e.reshape(WR // 8, 8, KP), axis=0)
        acc[q] = tot

    scores_slab(z)
    came = [(z + NZ - dz) % NZ for dz in FAR + NEAR]
    for i in range(len(FAR)):
        part = ph.at[came[i], colour, c]
        arrival(part, r_z.at[i]).wait_recv()
        for n, (dx, dy) in enumerate(NB):
            send(part, part, ("x2", i * len(NB) + n), r_n.at[i, n], plane_dev(plane(dx, dy)))

    def to_sibling(i):
        part = ph.at[came[i], :, c]
        return send(part, part, ("f", i), r_f.at[i], sibling)

    forwards = {}
    for i in (len(FAR), len(FAR) + 1):
        arrival(ph.at[came[i], :, c], r_z.at[i]).wait_recv()
        forwards[i] = to_sibling(i)
    for i in (len(FAR), len(FAR) + 1):
        forwards[i].wait_recv()
        scores_slab(came[i])
    for i in range(len(FAR) + 1):
        if i < len(FAR):
            for n, (dx, dy) in enumerate(NB):
                part = ph.at[came[i], (colour + 3 * NQ - dx - 2 * dy) % NQ, c]
                arrival(part, r_n.at[i, n]).wait_recv()
            forwards[i] = to_sibling(i)
        if i:
            forwards[i - 1].wait_recv()
            scores_slab(came[i - 1])

    lane = lax.broadcasted_iota(jnp.int32, (NT, 128), 1)
    row = lax.broadcasted_iota(jnp.int32, (NT, 128), 0)
    valid = lane + (row % LT) * 128 < KS

    def finish_column_sums(k):
        for q in range(NZ):
            part = jnp.sum(acc[q], axis=0, keepdims=True)
            for j in range(LT):
                vec[k, q * LT + j : q * LT + j + 1, :] = part[:, j * 128 : (j + 1) * 128]

    def reduce_columns(k, work_a, work_b):
        finish_column_sums(k)
        copies = []
        for i, (dx, dy) in enumerate(XY):
            copies.append(
                send(vec.at[k], buf_a.at[k, i], ("x1", i), r_a.at[k], plane_dev(plane(dx, dy)))
            )
        work_a()
        total = vec[k]
        arrival(buf_a.at[k], r_a.at[k]).wait_recv()
        for i in range(len(XY)):
            total = total + buf_a[k, i]
        vec_b[k] = total
        copies = []
        for i, dz in enumerate(ZO):
            copies.append(send(vec_b.at[k], buf_b.at[k, i], ("z1", i), r_b.at[k], z_dev(dz)))
        work_b()
        arrival(buf_b.at[k], r_b.at[k]).wait_recv()
        for i in range(len(ZO)):
            total = total + buf_b[k, i]
        csum[k] = jnp.where(valid, 1.0 / total, 0.0)

    def other_view():
        def step(q, carry):
            s = nt_dot(emb[2 * WR : 3 * WR, :], slab(q))
            ex[q, 2 * WR : 3 * WR, :] = jnp.exp(s * (1.0 / EPSILON_CODES))
            sc[q, WR : 2 * WR, :] = s
            return carry

        lax.fori_loop(0, NZ, step, 0)

    last = lax.broadcasted_iota(jnp.int32, (1, 128), 1) < KS - (LT - 1) * 128

    def denominators(first):
        R = 64

        def step(b, carry):
            rows = pl.ds(pl.multiple_of(first + b * R, R), R)
            total = jnp.zeros((R, 128), F32)
            for q in range(NZ):
                s = jnp.exp(sc[q, rows, :] * (1.0 / SOFTMAX_TEMPER))
                so[q, rows, :] = s
                for j in range(LT):
                    part = s[:, j * 128 : (j + 1) * 128]
                    if j == LT - 1:
                        part = jnp.where(last, part, 0.0)
                    total = total + part
            den[rows, :] = jnp.sum(total, axis=1, keepdims=True)
            return carry

        lax.fori_loop(0, WR // R, step, 0)

    def line_slot(dz):
        return (z + NZ + dz) % NZ

    def line_step(n):
        for i, way in enumerate((1, -1)):
            slot = line_slot(-way * (n - 1))
            part = emb_line.at[slot]
            if n == NZ // 2:
                part = emb_line.at[slot, pl.ds(i * WR, WR)]
            send(part, part, ("m", 2 + i), r_l.at[n - 1, i], z_dev(way % NZ))

    def line_wait(n):
        for i, way in enumerate((1, -1)):
            slot = line_slot(-way * n)
            part = emb_line.at[slot]
            if n == NZ // 2:
                part = emb_line.at[slot, pl.ds(i * WR, WR)]
            arrival(part, r_l.at[n - 1, i]).wait_recv()

    def line_scores(dz):
        slot = line_slot(dz)
        s = nt_dot(slab(z), emb_line[slot])
        so_line[slot] = jnp.exp(s * (1.0 / SOFTMAX_TEMPER))

    eye = lax.broadcasted_iota(jnp.int32, (128, 128), 0) == lax.broadcasted_iota(jnp.int32, (128, 128), 1)

    def to_lanes(ref, row):
        for i in range(2 * WR // 128):
            part = jnp.broadcast_to(ref[i * 128 : (i + 1) * 128, :], (128, 128))
            lanes[z, row + i : row + i + 1, :] = jnp.sum(jnp.where(eye, part, 0.0), axis=0, keepdims=True)

    def row_inverse(cs, rows, R):
        total = jnp.zeros((R, 128), F32)
        for q in range(NZ):
            for j in range(LT):
                t = q * LT + j
                total = total + ex[q, rows, j * 128 : (j + 1) * 128] * cs[t : t + 1, :]
        return 1.0 / jnp.sum(total, axis=1, keepdims=True)

    def sinkhorn_pass(k):
        R = 128
        acc[...] = jnp.zeros_like(acc)

        def step(b, carry):
            rows = pl.ds(pl.multiple_of(b * R, R), R)
            r = row_inverse(csum.at[k], rows, R)
            for q in range(NZ):
                t = ex[q, rows, :] * r
                acc[q] += jnp.sum(t.reshape(R // 8, 8, KP), axis=0)
            return carry

        lax.fori_loop(0, 2 * WR // R, step, 0)

    def nothing():
        pass

    emb_line[z, 0:WR, :] = emb[0:WR, :]
    emb_line[z, WR : 2 * WR, :] = emb[2 * WR : 3 * WR, :]

    def work_1a():
        line_step(1)
        other_view()
        line_scores(0)

    def work_2b():
        line_scores(-1)
        line_scores(1)
        to_lanes(den, 4)

    def work_3a():
        line_scores(-2)

    def work_1b():
        denominators(0)
        xt[:, 0:WR] = feats[c].astype(F32).T.astype(BF)

    def work_2a():
        denominators(WR)
        xt[:, WR : 2 * WR] = feats[o].astype(F32).T.astype(BF)

    reduce_columns(0, work_1a, work_1b)
    line_wait(1)
    line_step(2)
    sinkhorn_pass(0)
    reduce_columns(1, work_2a, work_2b)
    line_wait(2)
    line_step(3)
    sinkhorn_pass(1)
    reduce_columns(2, work_3a, lambda: line_scores(2))
    ccopy = send(csum.at[2], cothers, ("m", 1), r_c, sibling)
    line_wait(3)
    line_step(4)

    def row_scales(cs, row, erow):
        def step(b, carry):
            R = 128
            rows = pl.ds(pl.multiple_of(row + b * R, R), R)
            rsc[rows, :] = row_inverse(cs, pl.ds(pl.multiple_of(erow + b * R, R), R), R)
            return carry

        lax.fori_loop(0, WR // 128, step, 0)

    row_scales(csum.at[2], 0, 0)
    ccopy.wait_recv()
    row_scales(cothers, WR, 2 * WR)
    to_lanes(rsc, 0)
    for i, dz in enumerate(ZO):
        send(lanes.at[z], lanes.at[z], ("z1", i), r_v, z_dev(dz))

    RG = 32
    loss_acc[...] = jnp.zeros_like(loss_acc)

    def grad_step(b, carry):
        rows_c = pl.ds(pl.multiple_of(b * RG, RG), RG)
        rows_o = pl.ds(pl.multiple_of(WR + b * RG, RG), RG)
        erows_o = pl.ds(pl.multiple_of(2 * WR + b * RG, RG), RG)
        rc = rsc[rows_c, :] * gf
        ro = rsc[rows_o, :] * gf
        dc = gf / den[rows_c, :]
        do = gf / den[rows_o, :]
        total = jnp.zeros((RG, 128), F32)
        for q in range(NZ):
            for j in range(LT):
                t = q * LT + j
                cols = slice(j * 128, (j + 1) * 128)
                ac = ex[q, rows_c, cols] * csum[2, t : t + 1, :] * rc
                ao = ex[q, erows_o, cols] * cothers[t : t + 1, :] * ro
                gm[rows_c, t * 128 : (t + 1) * 128] = (so[q, rows_c, cols] * dc - ao).astype(BF)
                gm[rows_o, t * 128 : (t + 1) * 128] = (so[q, rows_o, cols] * do - ac).astype(BF)
                total = total + ao * sc[q, rows_c, cols] + ac * sc[q, rows_o, cols]
        loss_acc[...] += jnp.sum(total.reshape(RG // 8, 8, 128), axis=0)
        return carry

    lax.fori_loop(0, WR // RG, grad_step, 0)

    log_total = jnp.sum(jnp.log(den[...]))
    share = jnp.sum(loss_acc[...]) * (1.0 / (SOFTMAX_TEMPER * gf)) - log_total
    share_z[z] = jnp.full((8, 128), share, F32)
    for i, dz in enumerate(ZO):
        send(share_z.at[z], share_z.at[z], ("z2", i), r_h, z_dev(dz))

    eg[...] = dot(gm[...], ph[...].reshape(NZ * KP, D))
    along = jnp.sum(unit[...] * eg[...], axis=-1, keepdims=True)
    graw = ((eg[...] - unit[...] * along) * inv[...]).astype(BF)
    def half_rows(h, core):
        return pl.ds(pl.multiple_of((h * NC + core) * GQ, GQ), GQ)

    def own_rows(h, p):
        return pl.ds(pl.multiple_of((h * NC + c) * GQ + p * GR, GR), GR)

    wcopy = []
    for h in range(NH):
        theirs = half_rows(h, o)
        gw[theirs, :] = dot(xt[theirs, :], graw)
        wcopy.append(send(gw.at[theirs], buf_w.at[h], ("m", 6 + 2 * h), r_w.at[h], sibling))
    wcopies = []
    for h in range(NH):
        ours = half_rows(h, c)
        grads = dot(xt[ours, :], graw)
        wcopy[h].wait_recv()
        gw[ours, :] = grads + buf_w[h]
        for i, (dx, dy) in enumerate(XY):
            p = plane(dx, dy)
            wcopies.append(
                send(gw.at[own_rows(h, p)], buf_x.at[h, i], ("x1", i), r_wx.at[h], plane_dev(p))
            )

    for v, cs in enumerate((csum.at[2], cothers)):
        for j in range(LT):
            part = jnp.broadcast_to(cs[pl.ds(z * LT + j, 1), :], (128, 128))
            part = jnp.sum(jnp.where(eye, part, 0.0), axis=1, keepdims=True)
            col[v, j * 128 : (j + 1) * 128, :] = jnp.broadcast_to(part, (128, 128))
    line_scores(-3)
    line_scores(3)
    line_wait(4)
    line_scores(4)
    arrival(lanes.at[pl.ds(0, NZ - 1)], r_v).wait_recv()

    def line_grad(k, carry):
        scale = [lanes[k, i : i + 1, :] * gf for i in range(4)]
        soft = [gf / lanes[k, i : i + 1, :] for i in range(4, 8)]
        R = 32
        for b in range(KP // R):
            rows = slice(b * R, (b + 1) * R)
            for i in range(2):
                lc, lo = slice(i * 128, (i + 1) * 128), slice(WR + i * 128, WR + (i + 1) * 128)
                sc_, so_ = so_line[k, rows, lc], so_line[k, rows, lo]
                ac = sc_ * sc_ * col[0, rows, :] * scale[i]
                ao = so_ * so_ * col[1, rows, :] * scale[2 + i]
                gm_line[k, rows, lc] = (sc_ * soft[i] - ao).astype(BF)
                gm_line[k, rows, lo] = (so_ * soft[2 + i] - ac).astype(BF)
        return carry

    lax.fori_loop(0, NZ, line_grad, 0)
    grads = jnp.zeros((KP, D), F32)
    for k in range(NZ):
        grads = grads + dot(gm_line[k], emb_line[k])
    pg[...] = grads
    arrival(share_z.at[pl.ds(0, NZ - 1)], r_h).wait_recv()
    share = share_z[0, 0:1, 0:1]
    for k in range(1, NZ):
        share = share + share_z[k, 0:1, 0:1]
    spare = lax.broadcasted_iota(jnp.int32, (8, D), 0) == 7
    pg[KP - 8 : KP, :] = jnp.where(spare, share, pg[KP - 8 : KP, :])
    pcopy = send(pg.at[:, pl.ds(pl.multiple_of(o * DH, DH), DH)], buf_p, ("m", 4), r_p, sibling)
    pcopy.wait_recv()
    pr[...] = pg[:, pl.ds(pl.multiple_of(c * DH, DH), DH)] + buf_p[...]
    qcopies = []
    for i, (dx, dy) in enumerate(XY):
        p = plane(dx, dy)
        qcopies.append(
            send(pr.at[pl.ds(pl.multiple_of(p * PR_ROWS, PR_ROWS), PR_ROWS)], buf_q.at[i], ("x2", i), r_q, plane_dev(p))
        )

    for h in range(NH):
        total = gw[own_rows(h, me_p), :]
        arrival(buf_x.at[h], r_wx.at[h]).wait_recv()
        for i in range(len(XY)):
            total = total + buf_x[h, i]
        buf_y[h, z] = total
        for i, dz in enumerate(ZO):
            send(buf_y.at[h, z], buf_y.at[h, z], ("z1", i), r_wz.at[h], z_dev(dz))

    mine_p = pl.ds(pl.multiple_of(me_p * PR_ROWS, PR_ROWS), PR_ROWS)
    total = pr[mine_p, :]
    arrival(buf_q, r_q).wait_recv()
    for i in range(len(XY)):
        total = total + buf_q[i]
    fg[c, mine_p, :] = total
    for i, (dx, dy) in enumerate(XY):
        send(fg.at[c, mine_p], fg.at[c, mine_p], ("x2", i), r_qg, plane_dev(plane(dx, dy)))

    for h in range(NH):
        arrival(buf_y.at[h, pl.ds(0, NZ - 1)], r_wz.at[h]).wait_recv()
        total = buf_y[h, 0]
        for k in range(1, NZ):
            total = total + buf_y[h, k]
        part = own_rows(h, me_p)
        fw[part, :] = total
        for i, (dx, dy) in enumerate(XY):
            send(fw.at[part], fw.at[part], ("x1", i), r_wg.at[h], plane_dev(plane(dx, dy)))

    arrival(buf_q, r_qg).wait_recv()
    send(fg.at[c], fg.at[c], ("m", 5), r_qc, sibling).wait_recv()
    out_f = pltpu.make_async_copy(fg, gproto_out, s_in.at[0])
    out_f.start()

    forwards = []
    for h in range(NH):
        arrival(buf_x.at[h], r_wg.at[h]).wait_recv()
        part = fw.at[half_rows(h, c)]
        forwards.append(send(part, part, ("m", 7 + 2 * h), r_wc.at[h], sibling))
    for copy in forwards:
        copy.wait_recv()
    out_w = pltpu.make_async_copy(fw, gweight_out, s_in.at[1])
    out_w.start()
    out_f.wait()
    out_w.wait()

    for copy in pending.values():
        copy.wait_send()


def finish(batch_rows, fg, fw, protos, gproto_out, gweight_out, loss_out):
    g = jnp.concatenate([fg[0], fg[1]], axis=1)[0:KS, :]
    own = protos[...]
    pinv = lax.rsqrt(jnp.sum(own * own, axis=-1, keepdims=True) + TINY)
    u = own * pinv
    along = jnp.sum(u * g, axis=-1, keepdims=True)
    gproto_out[...] = (g - u * along) * pinv
    gweight_out[...] = fw[...]
    loss_out[...] = fg[0, KP - 1 : KP, 0:1] * (-1.0 / (2.0 * batch_rows))


def body(features, projection, prototypes):
    rows = features.shape[0]
    batch_rows = rows * lax.axis_size("dp")
    dma = pltpu.SemaphoreType.DMA
    nxy, nz = len(XY), len(ZO)
    vm = pltpu.VMEM
    scratch = [
        vm((WR, 2, E), BF), vm((2, WR, E), BF), vm((E, D), BF), vm((KS, D), F32), dma((3,)),
        vm((KP, D), F32), vm((NZ, NQ, NC, QR, D), BF), vm((2 * WR, D), F32), vm((2 * WR, 1), F32),
        vm((3 * WR, D), BF), vm((NZ, 2 * WR, D), BF), vm((E, 2 * WR), BF),
        vm((NZ, 3 * WR, KP), F32), vm((NZ, 2 * WR, KP), F32), vm((NZ, 2 * WR, KP), F32), vm((NZ, KP, 2 * WR), F32),
        vm((2 * WR, 1), F32), vm((2 * WR, 1), F32), vm((NZ, 8, KP), F32), vm((3, NT, 128), F32), vm((3, NT, 128), F32),
        vm((NT, 128), F32), vm((2 * WR, NZ * KP), BF),
        vm((3, nxy, NT, 128), F32), vm((3, nz, NT, 128), F32), vm((3, NT, 128), F32),
        vm((2 * WR, D), F32), vm((NZ, KP, 2 * WR), BF), vm((2, KP, 128), F32), vm((NZ, 8, 128), F32), vm((NZ, 8, 128), F32),
        vm((KP, D), F32), vm((KP, DH), F32), vm((KP, DH), F32), vm((nxy, PR_ROWS, DH), F32), vm((NC, KP, DH), F32),
        vm((E, D), F32), vm((NH, GQ, D), F32), vm((NH, nxy, GR, D), F32), vm((NH, NZ, GR, D), F32), vm((E, D), F32),
        vm((8, 128), F32),
        dma((nxy,)), dma((nxy,)), dma((nz,)), dma((nz,)), dma((nz,)), dma((6 + 2 * NH,)),
        dma((nz,)), dma((len(FAR), len(NB))), dma((nz,)), dma, dma((3,)), dma((3,)), dma, dma((4, 2)), dma,
        dma, dma, dma, dma, dma, dma((NH,)), dma((NH,)), dma((NH,)), dma((NH,)), dma((NH,)),
    ]
    vspec = pl.BlockSpec(memory_space=pltpu.VMEM)
    aspec = pl.BlockSpec(memory_space=pl.ANY)
    fg, fw = pl.pallas_call(
        functools.partial(kernel, batch_rows),
        out_shape=(
            jax.ShapeDtypeStruct((NC, KP, DH), F32),
            jax.ShapeDtypeStruct((E, D), F32),
        ),
        in_specs=[aspec] * 3,
        out_specs=(aspec,) * 2,
        scratch_shapes=scratch,
        compiler_params=pltpu.CompilerParams(
            collective_id=0, has_side_effects=True, vmem_limit_bytes=VLIM * 1024 * 1024
        ),
        name="swav",
    )(features, projection, prototypes)
    gproto, gweight, loss = pl.pallas_call(
        functools.partial(finish, batch_rows),
        out_shape=(
            jax.ShapeDtypeStruct((KS, D), F32),
            jax.ShapeDtypeStruct((E, D), F32),
            jax.ShapeDtypeStruct((1, 1), F32),
        ),
        in_specs=[vspec] * 3,
        out_specs=(vspec,) * 3,
        name="finish",
    )(fg, fw, prototypes)
    return gproto, gweight, loss.reshape(())


def solution(mesh):
    return jax.shard_map(
        body,
        mesh=mesh,
        in_specs=(P("dp", None, None), P(), P("mp", None)),
        out_specs=(P("mp", None), P(), P()),
        check_vma=False,
    )
```
